32 devices in a mesh: member: 4 (over z), space: 8 (over y, x, core).
Axes of the slice: x: 2, y: 2, z: 4, core: 2. Of those that a mesh axis runs over, the one named last changes fastest.
Arguments:
- latent_state: bfloat16 [32, 128, 640], P('space'), may hold values from -6 to 6
- member_noise: bfloat16 [8, 32, 128, 640], P('member', 'space'), may hold values from -6 to 6
- conv_weight: float32 [9, 640], replicated, may hold values from -2 to 2
- norm_gain: float32 [640], replicated, may hold values from 0.1 to 1.9
- weight_in: bfloat16 [1920, 640], replicated, may hold values from -0.25 to 0.25
- weight_down: bfloat16 [1920, 640], replicated, may hold values from -0.125 to 0.125
- weight_head: bfloat16 [640, 320], replicated, may hold values from -0.25 to 0.25
- target_field: float32 [32, 128, 320], P('space'), may hold values from -6 to 6
Outputs:
- grad_in: float32 [1920, 640], P(('member', 'space'))
- grad_down: float32 [1920, 640], P(('member', 'space'))
- grad_head: float32 [640, 320], replicated
- grad_gain: float32 [640], replicated
- grad_conv: float32 [9, 640], replicated
The draws below stay inside these ranges and needn't reach their ends.
All inputs are finite; a program needn't handle non-finite values.
Results may differ from the reference program's by a relative error of at most 0.007.
Values may be sent and summed in bfloat16 or wider, within the bound.
No kernel may reach another device: no remote copies, remote signals or barrier semaphores. Data moves between devices by JAX's collectives and lax.ppermute only.
A program may use at most 128 MiB of HBM per device.

```python
import math
import jax
import jax.numpy as jnp
from jax import lax

D = 640
FF = 1920
OUTC = 320
LON = 128
MEMBERS = 8
LAT = 32
POINTS = 4096


def level_of(rng, dims, shards, low, high):
    def one(axis_at, blocks):
        heights = jax.random.uniform(jax.random.fold_in(jax.random.fold_in(rng, 6), axis_at), (blocks,), jnp.float32, low / len(shards), high / len(shards))
        return jnp.repeat(jnp.exp(heights), dims[axis_at] // blocks).reshape((-1,) + (1,) * (len(dims) - axis_at - 1))

    level = one(*shards[0])
    for cut in shards[1:]:
        level = level * one(*cut)
    return level


def bell_draw(stream_key, dims, width, limit, cuts=(), kind=jnp.bfloat16):
    values = jax.random.normal(stream_key, dims, jnp.float32) * width
    if len(cuts) > 0:
        values = level_of(stream_key, dims, cuts, -0.22, 0.18) * values
    return jnp.clip(values, min=-limit, max=limit).astype(kind)


def setup_inputs(seed: int = 0) -> dict:
    keys = jax.random.split(jax.random.key(seed), 9)
    latent_state = bell_draw(keys[0], (LAT, LON, D), 1.0, 6.0, ((0, 8),))
    member_noise = bell_draw(keys[1], (MEMBERS, LAT, LON, D), 1.0, 6.0, ((0, 4), (1, 8)))
    conv_weight = bell_draw(keys[2], (9, D), 9 ** -0.5, 2.0, (), jnp.float32)
    norm_gain = jnp.clip(1.0 + 0.18 * jax.random.normal(keys[3], (D,), jnp.float32), 0.1, 1.9)
    weight_in = bell_draw(keys[4], (FF, D), D ** -0.5, 0.25)
    weight_down = bell_draw(keys[5], (FF, D), FF ** -0.5, 0.125)
    weight_head = bell_draw(keys[6], (D, OUTC), D ** -0.5, 0.25)
    target_field = bell_draw(keys[7], (LAT, LON, OUTC), 1.0, 6.0, ((0, 8),), jnp.float32)
    return dict(latent_state=latent_state, member_noise=member_noise, conv_weight=conv_weight, norm_gain=norm_gain, weight_in=weight_in, weight_down=weight_down, weight_head=weight_head, target_field=target_field)


def pair_pull(own_pred, every_pred):
    gram = jnp.einsum('apc,bpc->abp', own_pred, every_pred, precision=lax.Precision.HIGHEST)
    own_sq = lax.optimization_barrier(jnp.sum(own_pred * own_pred, axis=-1))
    every_sq = lax.optimization_barrier(jnp.sum(every_pred * every_pred, axis=-1))
    inverse = 1.0 / jnp.sqrt(own_sq[:, None, :] + every_sq[None, :, :] - 2.0 * gram + 1.0)
    weight_sum = lax.optimization_barrier(jnp.sum(inverse, axis=1))
    pulled = jnp.einsum('abp,bpc->apc', inverse, every_pred, precision=lax.Precision.HIGHEST)
    return own_pred * weight_sum[..., None] - pulled

def reference(latent_state, member_noise, conv_weight, norm_gain, weight_in, weight_down, weight_head, target_field):
    mixed = (latent_state[None].astype(jnp.float32) + member_noise.astype(jnp.float32)).astype(jnp.bfloat16)
    padded = jnp.pad(mixed, ((0, 0), (1, 1), (0, 0), (0, 0)))
    shifted = [jnp.roll(padded[:, offa:offa + LAT], 1 - offb, axis=2) for offa in range(3) for offb in range(3)]
    conv_out = jnp.zeros(mixed.shape, jnp.float32)
    for index in range(9):
        conv_out = conv_out + conv_weight[index] * shifted[index].astype(jnp.float32)
    total_rows = MEMBERS * POINTS
    conv_rows = conv_out.reshape(total_rows, D)
    center = conv_rows - lax.optimization_barrier(jnp.mean(conv_rows, axis=-1, keepdims=True))
    inv_std = lax.rsqrt(lax.optimization_barrier(jnp.mean(center * center, axis=-1, keepdims=True)) + 1e-05)
    normal = center * inv_std
    normed_b = (normal * norm_gain).astype(jnp.bfloat16)
    contract_last = (((1,), (1,)), ((), ()))
    contract_first = (((0,), (0,)), ((), ()))
    pre_act = lax.dot_general(normed_b, weight_in, contract_last, preferred_element_type=jnp.float32)
    activ_b = jax.nn.gelu(pre_act).astype(jnp.bfloat16)
    hidden_b = (mixed.reshape(total_rows, D).astype(jnp.float32) + jnp.dot(activ_b, weight_down, preferred_element_type=jnp.float32)).astype(jnp.bfloat16)
    predict = jnp.dot(hidden_b, weight_head, preferred_element_type=jnp.float32).reshape(MEMBERS, POINTS, OUTC)
    loss_scale = math.sqrt(MEMBERS * OUTC / POINTS)
    error = predict - target_field.reshape(1, POINTS, OUTC)
    dist_target = jnp.sqrt(lax.optimization_barrier(jnp.sum(error * error, axis=-1, keepdims=True)) + 1.0)
    attract = error / dist_target / MEMBERS
    repulse = pair_pull(predict, predict)
    grad_pred = loss_scale * (attract - repulse / (MEMBERS * (MEMBERS - 1)))
    grad_b = grad_pred.reshape(total_rows, OUTC).astype(jnp.bfloat16)
    grad_head = lax.dot_general(hidden_b, grad_b, contract_first, preferred_element_type=jnp.float32)
    ghid_b = lax.dot_general(grad_b, weight_head, contract_last, preferred_element_type=jnp.float32).astype(jnp.bfloat16)
    grad_down = lax.dot_general(activ_b, ghid_b, contract_first, preferred_element_type=jnp.float32)
    grad_act = lax.dot_general(ghid_b, weight_down, contract_last, preferred_element_type=jnp.float32)
    grad_pre = jax.vjp(jax.nn.gelu, pre_act)[1](grad_act)[0]
    gpre_b = grad_pre.astype(jnp.bfloat16)
    grad_in = lax.dot_general(gpre_b, normed_b, contract_first, preferred_element_type=jnp.float32)
    grad_normed = jnp.dot(gpre_b, weight_in, preferred_element_type=jnp.float32)
    grad_gain = lax.optimization_barrier(jnp.sum(grad_normed * normal, axis=0))
    scaled = grad_normed * norm_gain
    grad_conv_out = (scaled - lax.optimization_barrier(jnp.mean(scaled, axis=-1, keepdims=True)) - normal * lax.optimization_barrier(jnp.mean(scaled * normal, axis=-1, keepdims=True))) * inv_std
    grad_conv4 = grad_conv_out.reshape(mixed.shape)
    grad_conv = jnp.stack([lax.optimization_barrier(jnp.sum(shifted[index].astype(jnp.float32) * grad_conv4, axis=(0, 1, 2))) for index in range(9)])
    return (grad_in, grad_down, grad_head, grad_gain, grad_conv)
```

```python
import math

import jax
import jax.numpy as jnp
from jax import lax
from jax.experimental import pallas as pl
from jax.experimental.pallas import tpu as pltpu
from jax.sharding import PartitionSpec as P


F32 = jnp.float32
BF16 = jnp.bfloat16


def ring(count, step):
    return [(i, (i + step) % count) for i in range(count)]


def flip(count, bit):
    return [(i, i ^ bit) for i in range(count)]


def halo(edges_low, edges_high):
    count = lax.axis_size("space")
    above = lax.ppermute(edges_high, "space", [(i, i + 1) for i in range(count - 1)])
    below = lax.ppermute(edges_low, "space", [(i + 1, i) for i in range(count - 1)])
    return above, below


def pair_kernel(*refs):
    half = len(refs) // 2
    ins, outs = refs[:half], refs[half:]
    per = ins[0].shape[0]
    rows = [(ref, m) for ref in ins for m in range(per)]
    values = [ref[m].astype(F32) for ref, m in rows]
    pulls = [None] * len(values)
    for a in range(len(values)):
        for b in range(a + 1, len(values)):
            gap = values[a] - values[b]
            weight = lax.rsqrt(jnp.sum(gap * gap, axis=-1, keepdims=True) + 1.0)
            pull = gap * weight
            pulls[a] = pull if pulls[a] is None else pulls[a] + pull
            pulls[b] = -pull if pulls[b] is None else pulls[b] - pull
    for index, pull in enumerate(pulls):
        outs[index // per][index % per] = pull.astype(BF16)


def pair_pull(groups):
    per, points, width = groups[0].shape
    tile = 16 if points % 16 == 0 else points
    spec = pl.BlockSpec((per, tile, width), lambda i: (0, i, 0))
    return pl.pallas_call(
        pair_kernel,
        grid=(points // tile,),
        in_specs=[spec] * len(groups),
        out_specs=[spec] * len(groups),
        out_shape=[jax.ShapeDtypeStruct(groups[0].shape, BF16)] * len(groups),
        name="pair",
    )(*groups)


def pick(array, index, axis):
    return lax.dynamic_index_in_dim(array, index, axis=axis, keepdims=False)


def exchange(array, axis, count, bit, where):
    mine = (lax.axis_index(axis) // bit) % 2
    send = pick(array, 1 - mine, where).astype(BF16)
    return pick(array, mine, where).astype(F32) + lax.ppermute(send, axis, flip(count, bit)).astype(
        F32
    )


def scatter_sum(blocks):
    members = lax.axis_size("member")
    spaces = lax.axis_size("space")
    bits = spaces.bit_length() - 1
    rows, width = blocks.shape[1:]
    view = blocks.reshape((members,) + (2,) * bits + (rows, width))
    first = exchange(view, "space", spaces, 1, bits)
    cut = rows // 2
    parts = []
    for flow in range(2):
        part = lax.slice_in_dim(first, flow * cut, flow * cut + cut, axis=first.ndim - 2)
        left = list(range(1, bits))
        for level in left if flow == 0 else left[::-1]:
            where = 1 + sum(1 for other in left if other > level and part.ndim > 0 and other in live(left, level, flow))
            part = exchange(part, "space", spaces, 1 << level, where)
        parts.append(part)
    mine = jnp.concatenate(parts, axis=1)
    me = lax.axis_index("member")
    total = pick(mine, me, 0)
    half = mine.astype(BF16)
    for step in range(1, members):
        sent = pick(half, (me + step) % members, 0)
        total = total + lax.ppermute(sent, "member", ring(members, step)).astype(F32)
    return total


def live(left, level, flow):
    order = left if flow == 0 else left[::-1]
    return order[order.index(level) :]


def gather_all(shard):
    members = lax.axis_size("member")
    spaces = lax.axis_size("space")
    me = lax.axis_index("member")
    pieces = [shard] + [
        lax.ppermute(shard, "member", ring(members, members - step)) for step in range(1, members)
    ]
    stack = jnp.stack(pieces)
    whole = lax.dynamic_slice_in_dim(jnp.concatenate([stack, stack]), members - me, members, 0)
    bit = spaces // 2
    whole = whole[:, None]
    levels = []
    while bit:
        levels.append(bit)
        bit //= 2
    for bit in levels:
        other = lax.ppermute(whole, "space", flip(spaces, bit))
        mine = (lax.axis_index("space") // bit) % 2
        low = jnp.where(mine == 0, whole, other)
        high = jnp.where(mine == 0, other, whole)
        whole = jnp.stack([low, high], axis=2).reshape(
            (members, whole.shape[1] * 2) + whole.shape[2:]
        )
    return whole


def sum_all(array):
    members = lax.axis_size("member")
    spaces = lax.axis_size("space")
    bit = 1
    while bit < spaces:
        array = array + lax.ppermute(array, "space", flip(spaces, bit))
        bit *= 2
    bit = 1
    while bit < members:
        array = array + lax.ppermute(array, "member", flip(members, bit))
        bit *= 2
    return array


def body(
    latent_state,
    member_noise,
    conv_weight,
    norm_gain,
    weight_in,
    weight_down,
    weight_head,
    target_field,
):
    mem_dev, lat_dev, lon_len, width = member_noise.shape
    out_width = weight_head.shape[1]
    members = lax.axis_size("member")
    spaces = lax.axis_size("space")
    devices = members * spaces
    members_all = mem_dev * members
    points_all = lat_dev * spaces * lon_len
    cells_dev = lat_dev * lon_len
    total_rows = mem_dev * cells_dev
    loss_scale = math.sqrt(members_all * out_width / points_all)
    me = lax.axis_index("member")
    units = weight_in.shape[0] // devices
    unit_pad = -(-units // 16) * 16

    def padded_rows(weight):
        view = weight.reshape(devices, units, width)
        return jnp.pad(view, ((0, 0), (0, unit_pad - units), (0, 0))).reshape(-1, width)

    mixed = (latent_state[None].astype(F32) + member_noise.astype(F32)).astype(BF16)
    above, below = halo(mixed[:, :1], mixed[:, -1:])
    weight_in = padded_rows(weight_in)
    weight_down = padded_rows(weight_down)
    padded = jnp.concatenate([above, mixed, below], axis=1)
    shifted = [
        jnp.roll(padded[:, offa : offa + lat_dev], 1 - offb, axis=2)
        for offa in range(3)
        for offb in range(3)
    ]
    conv_out = jnp.zeros(mixed.shape, F32)
    for index in range(9):
        conv_out = conv_out + conv_weight[index] * shifted[index].astype(F32)
    conv_rows = conv_out.reshape(total_rows, width)
    center = conv_rows - jnp.mean(conv_rows, axis=-1, keepdims=True)
    inv_std = lax.rsqrt(jnp.mean(center * center, axis=-1, keepdims=True) + 1e-05)
    normal = center * inv_std
    normed_b = (normal * norm_gain).astype(BF16)
    contract_last = (((1,), (1,)), ((), ()))
    contract_first = (((0,), (0,)), ((), ()))
    pre_act = lax.dot_general(normed_b, weight_in, contract_last, preferred_element_type=F32)
    activ_b = jax.nn.gelu(pre_act).astype(BF16)
    hidden_b = (
        mixed.reshape(total_rows, width).astype(F32)
        + jnp.dot(activ_b, weight_down, preferred_element_type=F32)
    ).astype(BF16)
    predict = jnp.dot(hidden_b, weight_head, preferred_element_type=F32).reshape(
        mem_dev, cells_dev, out_width
    )
    sendable = predict.astype(BF16).reshape(mem_dev, members, cells_dev // members, out_width)
    groups = [pick(sendable, me, 1)] + [
        lax.ppermute(pick(sendable, (me + k) % members, 1), "member", ring(members, k))
        for k in range(1, members)
    ]
    error = predict - target_field.reshape(1, cells_dev, out_width)
    dist_target = jnp.sqrt(jnp.sum(error * error, axis=-1, keepdims=True) + 1.0)
    attract = error / dist_target / members_all
    pulls = pair_pull(groups)
    back = jnp.stack(
        [pulls[0]]
        + [
            lax.ppermute(pulls[k], "member", ring(members, members - k)) for k in range(1, members)
        ],
        axis=1,
    )
    repulse = lax.dynamic_slice_in_dim(
        jnp.concatenate([back, back], axis=1), members - me, members, axis=1
    ).reshape(mem_dev, cells_dev, out_width)
    grad_pred = loss_scale * (attract - repulse.astype(F32) / (members_all * (members_all - 1)))
    grad_b = grad_pred.reshape(total_rows, out_width).astype(BF16)
    head_local = lax.dot_general(grad_b, hidden_b, contract_first, preferred_element_type=F32)
    ghid_b = lax.dot_general(
        grad_b, weight_head, contract_last, preferred_element_type=F32
    ).astype(BF16)
    down_part = lax.dot_general(activ_b, ghid_b, contract_first, preferred_element_type=F32)

    head_rows = -(-out_width // devices)
    head_blocks = jnp.pad(
        head_local, ((0, devices * head_rows - out_width), (0, 0))
    ).reshape(devices, head_rows, width)
    down_blocks = jnp.concatenate(
        [down_part.reshape(devices, unit_pad, width), jnp.pad(head_blocks, ((0, 0), (0, 16 - head_rows), (0, 0)))],
        axis=1,
    )
    down_mine = scatter_sum(down_blocks)
    head_mine = down_mine[unit_pad : unit_pad + head_rows].astype(BF16)
    head_total = gather_all(head_mine).reshape(-1, width)[:out_width].T.astype(F32)

    grad_act = lax.dot_general(ghid_b, weight_down, contract_last, preferred_element_type=F32)
    grad_pre = jax.vjp(jax.nn.gelu, pre_act)[1](grad_act)[0]
    gpre_b = grad_pre.astype(BF16)
    in_part = lax.dot_general(gpre_b, normed_b, contract_first, preferred_element_type=F32)
    in_mine = scatter_sum(in_part.reshape(devices, unit_pad, width))
    grad_normed = jnp.dot(gpre_b, weight_in, preferred_element_type=F32)
    gain_local = jnp.sum(grad_normed * normal, axis=0)
    scaled = grad_normed * norm_gain
    grad_conv_out = (
        scaled
        - jnp.mean(scaled, axis=-1, keepdims=True)
        - normal * jnp.mean(scaled * normal, axis=-1, keepdims=True)
    ) * inv_std
    grad_conv4 = grad_conv_out.reshape(mixed.shape)
    small = jnp.stack(
        [
            jnp.sum(shifted[index].astype(F32) * grad_conv4, axis=(0, 1, 2))
            for index in range(9)
        ]
        + [gain_local]
    )
    small = sum_all(small)
    return (in_mine[:units], down_mine[:units], head_total, small[9], small[:9])


def solution(mesh):
    return jax.shard_map(
        body,
        mesh=mesh,
        in_specs=(
            P("space", None, None),
            P("member", "space", None, None),
            P(),
            P(),
            P(),
            P(),
            P(),
            P("space", None, None),
        ),
        out_specs=(P(("member", "space"), None), P(("member", "space"), None), P(), P(), P()),
        check_vma=False,
    )
```

```python
import functools
import math

import jax
import jax.numpy as jnp
from jax import lax
from jax.experimental import pallas as pl
from jax.experimental.pallas import tpu as pltpu
from jax.sharding import PartitionSpec as P


F32 = jnp.float32
BF16 = jnp.bfloat16
LAST = (((1,), (1,)), ((), ()))
FIRST = (((0,), (0,)), ((), ()))
SMEM = pl.BlockSpec(memory_space=pltpu.SMEM)


def dot(left, right, dims=(((1,), (0,)), ((), ()))):
    return lax.dot_general(left, right, dims, preferred_element_type=F32)


def ring(count, step):
    return [(i, (i + step) % count) for i in range(count)]


def flip(count, bit):
    return [(i, i ^ bit) for i in range(count)]


def call(kernel, ins, outs, scratch, name, scalars=0):
    return pl.pallas_call(
        kernel,
        in_specs=[SMEM] * scalars
        + [pl.BlockSpec(memory_space=pltpu.VMEM)] * (len(ins) - scalars),
        out_specs=[pl.BlockSpec(memory_space=pltpu.VMEM)] * len(outs),
        out_shape=[jax.ShapeDtypeStruct(shape, kind) for shape, kind in outs],
        scratch_shapes=scratch,
        name=name,
    )(*ins)


def tile_of(total):
    return next(t for t in range(640, 0, -128) if total % t == 0)


def mixed_row(noise, latent, edges, m, i):
    if i < 0:
        return edges[0][m, 0]
    if i >= latent.shape[0]:
        return edges[1][m, 0]
    return (latent[i].astype(F32) + noise[m, i].astype(F32)).astype(BF16)


def forward_kernel(rows, members, members_all, edged, *refs):
    me_ref, noise, latent = refs[:3]
    edges = refs[3:5] if edged else ()
    conv_w, gain, w_in, w_down, w_head, target = refs[3 + len(edges) : 9 + len(edges)]
    rest = refs[9 + len(edges) :]
    normed, normal, inv, activ, slope, hidden, attract = rest[:7]
    sends = rest[7 : 7 + members]
    mix_s, acc, pred = rest[7 + members :]
    mem_dev, _, lon, width = noise.shape
    span = len(rows) * lon
    tile = tile_of(w_in.shape[0])
    me = me_ref[0]

    def conv_step(m, carry):
        for at, i in enumerate(rows):
            start = pl.multiple_of(m * span + at * lon, lon)
            here = pl.ds(start, lon)
            sums = [None] * 3
            for a in range(3):
                row_b = mixed_row(noise, latent, edges, m, i + a - 1)
                if a == 1:
                    mix_s[here, :] = row_b
                row = row_b.astype(F32)
                for b in range(3):
                    k = 3 * a + b
                    term = conv_w[k : k + 1, :] * row
                    sums[b] = term if sums[b] is None else sums[b] + term
            conv = (
                sums[1] + pltpu.roll(sums[0], 1, axis=0) + pltpu.roll(sums[2], lon - 1, axis=0)
            )
            center = conv - jnp.mean(conv, axis=-1, keepdims=True)
            scale = lax.rsqrt(jnp.mean(center * center, axis=-1, keepdims=True) + 1e-05)
            unit = center * scale
            normal[here, :] = unit
            inv[here, :] = jnp.broadcast_to(scale, (lon, 128))
            normed[here, :] = (unit * gain[...]).astype(BF16)
        return carry

    lax.fori_loop(0, mem_dev, conv_step, 0)
    acc[...] = jnp.zeros(acc.shape, F32)

    def unit_step(t, carry):
        at = pl.ds(pl.multiple_of(t * tile, tile), tile)
        x = dot(normed[...], w_in[at, :], LAST)
        rate = math.sqrt(2.0 / math.pi)
        square = x * x
        tanh = jnp.tanh(rate * x * (1.0 + 0.044715 * square))
        cdf = 0.5 + 0.5 * tanh
        act = (x * cdf).astype(BF16)
        activ[:, at] = act
        slope[:, at] = (
            cdf + 0.5 * x * (1.0 - tanh * tanh) * (rate * (1.0 + (3 * 0.044715) * square))
        ).astype(BF16)
        acc[...] += dot(act, w_down[at, :])
        return carry

    lax.fori_loop(0, w_in.shape[0] // tile, unit_step, 0)
    hid = (mix_s[...].astype(F32) + acc[...]).astype(BF16)
    hidden[...] = hid
    pred[...] = dot(hid, w_head[...])
    for m in range(mem_dev):
        for at, i in enumerate(rows):
            here = pl.ds(m * span + at * lon, lon)
            error = pred[here, :] - target[i]
            dist = lax.rsqrt(jnp.sum(error * error, axis=-1, keepdims=True) + 1.0)
            attract[here, :] = error * dist * (1.0 / members_all)
    points = span // members
    for k in range(members):
        chunk = lax.rem(me + k, members)
        for m in range(mem_dev):
            at = pl.ds(pl.multiple_of(m * span + chunk * points, points), points)
            sends[k][m] = pred[at, :].astype(BF16)


def forward(me, noise, latent, edges, conv_w, gain, w_in, w_down, w_head, target, rows, members):
    mem_dev, _, lon, width = noise.shape
    out_width = w_head.shape[1]
    units = w_in.shape[0]
    total = mem_dev * len(rows) * lon
    points = len(rows) * lon // members
    ins = [me, noise, latent, *edges, conv_w, gain, w_in, w_down, w_head, target]
    outs = [
        ((total, width), BF16),
        ((total, width), F32),
        ((total, 128), F32),
        ((total, units), BF16),
        ((total, units), BF16),
        ((total, width), BF16),
        ((total, out_width), F32),
    ] + [((mem_dev, points, out_width), BF16)] * members
    scratch = [
        pltpu.VMEM((total, width), BF16),
        pltpu.VMEM((total, width), F32),
        pltpu.VMEM((total, out_width), F32),
    ]
    kernel = functools.partial(
        forward_kernel, rows, members, members * mem_dev, len(edges) > 0
    )
    out = call(kernel, ins, outs, scratch, "forward", 1)
    return out[:7], out[7:]


def pair_kernel(*refs):
    half = len(refs) // 2
    ins, outs = refs[:half], refs[half:]
    per, points = ins[0].shape[:2]
    step = 16 if points % 16 == 0 else points

    def run(t, carry):
        at = pl.ds(pl.multiple_of(t * step, step), step)
        values = [ref[m, at, :].astype(F32) for ref in ins for m in range(per)]
        pulls = [None] * len(values)
        for a in range(len(values)):
            for b in range(a + 1, len(values)):
                gap = values[a] - values[b]
                pull = gap * lax.rsqrt(jnp.sum(gap * gap, axis=-1, keepdims=True) + 1.0)
                pulls[a] = pull if pulls[a] is None else pulls[a] + pull
                pulls[b] = -pull if pulls[b] is None else pulls[b] - pull
        for index, pull in enumerate(pulls):
            outs[index // per][index % per, at, :] = pull.astype(BF16)
        return carry

    lax.fori_loop(0, points // step, run, 0)


def pair_pull(groups):
    return call(pair_kernel, groups, [(groups[0].shape, BF16)] * len(groups), [], "pair")


def slope_kernel(members, scale, share, *refs):
    me_ref, attract = refs[:2]
    pulls = refs[2 : 2 + members]
    w_head, w_down, slope, grad, ghid, gpre = refs[2 + members :]
    mem_dev, points, _ = pulls[0].shape
    span = attract.shape[0] // mem_dev
    tile = tile_of(w_down.shape[0])
    me = me_ref[0]
    for k in range(members):
        chunk = lax.rem(me + k, members)
        for m in range(mem_dev):
            at = pl.ds(pl.multiple_of(m * span + chunk * points, points), points)
            grad[at, :] = (scale * (attract[at, :] - pulls[k][m].astype(F32) * share)).astype(BF16)
    ghid[...] = dot(grad[...], w_head[...], LAST).astype(BF16)

    def unit_step(t, carry):
        at = pl.ds(pl.multiple_of(t * tile, tile), tile)
        back = dot(ghid[...], w_down[at, :], LAST)
        gpre[:, at] = (slope[:, at].astype(F32) * back).astype(BF16)
        return carry

    lax.fori_loop(0, w_down.shape[0] // tile, unit_step, 0)


def slopes(me, attract, pulls, w_head, w_down, slope, scale, share):
    total, out_width = attract.shape
    outs = [
        ((total, out_width), BF16),
        ((total, w_head.shape[0]), BF16),
        (slope.shape, BF16),
    ]
    kernel = functools.partial(slope_kernel, len(pulls), scale, share)
    ins = [me, attract, *pulls, w_head, w_down, slope]
    return call(kernel, ins, outs, [], "slopes", 1)


def norm_kernel(rows, edged, *refs):
    gpre, w_in, normal, inv, gain, noise, latent = refs[:7]
    edges = refs[7:9] if edged else ()
    small, acc = refs[7 + len(edges) :]
    mem_dev, _, lon, width = noise.shape
    span = len(rows) * lon
    tile = tile_of(w_in.shape[0])
    acc[...] = jnp.zeros(acc.shape, F32)

    def unit_step(t, carry):
        at = pl.ds(pl.multiple_of(t * tile, tile), tile)
        acc[...] += dot(gpre[:, at], w_in[at, :])
        return carry

    lax.fori_loop(0, w_in.shape[0] // tile, unit_step, 0)
    small[...] = jnp.zeros(small.shape, F32)

    def conv_step(m, carry):
        for at, i in enumerate(rows):
            here = pl.ds(pl.multiple_of(m * span + at * lon, lon), lon)
            back = acc[here, :]
            unit = normal[here, :]
            product = back * unit
            small[9:10, :] += jnp.sum(product, axis=0, keepdims=True)
            g = back * gain[...]
            mean = jnp.mean(g, axis=-1, keepdims=True)
            along = jnp.mean(product * gain[...], axis=-1, keepdims=True)
            out = (g - mean - unit * along) * inv[here, 0:1]
            turned = [pltpu.roll(out, lon - 1, axis=0), out, pltpu.roll(out, 1, axis=0)]
            for a in range(3):
                row = mixed_row(noise, latent, edges, m, i + a - 1).astype(F32)
                for b in range(3):
                    k = 3 * a + b
                    small[k : k + 1, :] += jnp.sum(row * turned[b], axis=0, keepdims=True)
        return carry

    lax.fori_loop(0, mem_dev, conv_step, 0)


def norms(gpre, w_in, normal, inv, gain, noise, latent, edges, rows):
    width = w_in.shape[1]
    ins = [gpre, w_in, normal, inv, gain, noise, latent, *edges]
    kernel = functools.partial(norm_kernel, rows, len(edges) > 0)
    scratch = [pltpu.VMEM(normal.shape, F32)]
    return call(kernel, ins, [((16, width), F32)], scratch, "norms")[0]


def weight_kernel(units, unit_pad, head_rows, *refs):
    bit_ref = refs[0]
    count = 4 if head_rows == 0 else 8
    ins = refs[1 : 1 + count]
    keep, send, acc = refs[1 + count : 4 + count]
    left = ins[0:2]
    right = ins[2:4]
    size = left[0].shape[1]
    tile = tile_of(size)

    def step(t, carry):
        at = pl.ds(pl.multiple_of(t * tile, tile), tile)
        acc[at, :] = dot(left[0][:, at], right[0][...], FIRST) + dot(
            left[1][:, at], right[1][...], FIRST
        )
        return carry

    lax.fori_loop(0, size // tile, step, 0)
    acc[size:, :] = jnp.zeros((acc.shape[0] - size, acc.shape[1]), F32)
    low = bit_ref[0] == 0
    head = None
    if head_rows:
        head = refs[4 + count]
        grads, hids = ins[4:6], ins[6:8]
        wide = grads[0].shape[1]
        head[0:wide, :] = dot(grads[0][...], hids[0][...], FIRST) + dot(
            grads[1][...], hids[1][...], FIRST
        )
        head[wide:, :] = jnp.zeros((head.shape[0] - wide, head.shape[1]), F32)

    def emit(source, j, rows, per, first):
        even = source[2 * j * per : 2 * j * per + rows, :]
        odd = source[(2 * j + 1) * per : (2 * j + 1) * per + rows, :]
        keep[j, first : first + rows, :] = jnp.where(low, even, odd)
        send[j, first : first + rows, :] = jnp.where(low, odd, even).astype(BF16)

    for j in range(keep.shape[0]):
        emit(acc, j, unit_pad, units, 0)
        if head_rows:
            emit(head, j, keep.shape[1] - unit_pad, head_rows, unit_pad)


def pad_to(value, unit):
    return -(-value // unit) * unit


def weights(bit, left, right, devices, head=()):
    size = left[0].shape[1]
    width = right[0].shape[1]
    units = size // devices
    unit_pad = pad_to(units, 16)
    rows = unit_pad
    head_rows = 0
    scratch = [pltpu.VMEM((pad_to(size + unit_pad - units, 8) + 8, width), F32)]
    if head:
        head_rows = -(-head[0].shape[1] // devices)
        extra = pad_to(head_rows, 16)
        rows += extra
        scratch.append(pltpu.VMEM((pad_to(devices * head_rows + extra, 8) + 8, width), F32))
    ins = [bit, *left, *right, *head]
    outs = [((devices // 2, rows, width), F32), ((devices // 2, rows, width), BF16)]
    kernel = functools.partial(weight_kernel, units, unit_pad, head_rows)
    return call(kernel, ins, outs, scratch, "weights", 1)


def insert(index, place, bit):
    low = (1 << place) - 1
    return ((index >> place) << (place + 1)) | (bit << place) | (index & low)


def merge_kernel(plans, bits_ref, *refs):
    count = len(plans)
    keeps, gots = refs[:count], refs[count : 2 * count]
    outs = refs[2 * count :]
    for flow, (first, rows, place, which) in enumerate(plans):
        bit = bits_ref[which]
        keep, got = keeps[flow], gots[flow]
        out_keep, out_send = outs[2 * flow : 2 * flow + 2]
        at = pl.ds(first, rows)

        def step(i, carry, keep=keep, got=got, out_keep=out_keep, out_send=out_send, at=at, place=place, bit=bit):
            mine = insert(i, place, bit)
            other = insert(i, place, 1 - bit)
            out_keep[i] = keep[mine, at, :] + got[mine, at, :].astype(F32)
            out_send[i] = (keep[other, at, :] + got[other, at, :].astype(F32)).astype(BF16)
            return carry

        lax.fori_loop(0, out_keep.shape[0], step, 0)


def merge(bits, keeps, gots, plans):
    width = keeps[0].shape[2]
    outs = []
    for keep, (_, rows, _, _) in zip(keeps, plans):
        blocks = keep.shape[0] // 2
        outs += [((blocks, rows, width), F32), ((blocks, rows, width), BF16)]
    kernel = functools.partial(merge_kernel, plans)
    out = call(kernel, [bits, *keeps, *gots], outs, [], "merge", 1)
    return out[0::2], out[1::2]


def turn_kernel(members, firsts, me_ref, *refs):
    count = len(firsts)
    keeps, gots = refs[:count], refs[count : 2 * count]
    outs = refs[2 * count :]
    for k in range(members):
        block = lax.rem(me_ref[0] + k, members)
        for flow, first in enumerate(firsts):
            value = keeps[flow][block] + gots[flow][block].astype(F32)
            outs[k][first : first + value.shape[0], :] = value.astype(outs[k].dtype)


def turn(me, keeps, gots, members):
    width = keeps[0].shape[2]
    firsts, rows = [], 0
    for keep in keeps:
        firsts.append(rows)
        rows += keep.shape[1]
    outs = [((rows, width), F32)] + [((rows, width), BF16)] * (members - 1)
    kernel = functools.partial(turn_kernel, members, tuple(firsts))
    return call(kernel, [me, *keeps, *gots], outs, [], "turn", 1)


def reduce_blocks(me, bits, keep, send):
    members = lax.axis_size("member")
    spaces = lax.axis_size("space")
    levels = list(range(1, spaces.bit_length() - 1))
    got = lax.ppermute(send, "space", flip(spaces, 1))
    rows = keep.shape[1]
    cut = pad_to(rows, 32) // 2
    flows = [(0, cut, levels)] + ([(cut, rows - cut, levels[::-1])] if rows > cut else [])
    keeps, gots = [keep] * len(flows), [got] * len(flows)
    for depth in range(len(levels)):
        plans = []
        for first, size, order in flows:
            live = order[depth:]
            place = sum(1 for other in live if other < live[0])
            plans.append((first if depth == 0 else 0, size, place, order[depth]))
        keeps, sends = merge(bits, keeps, gots, tuple(plans))
        gots = [
            lax.ppermute(part, "space", flip(spaces, 1 << order[depth]))
            for part, (_, _, order) in zip(sends, flows)
        ]
    parts = turn(me, keeps, gots, members)
    return parts[0], [
        lax.ppermute(parts[k], "member", ring(members, k)) for k in range(1, members)
    ]


def add_up(own, others):
    for other in others:
        own = own + other.astype(F32)
    return own


def gather_all(shard):
    members = lax.axis_size("member")
    spaces = lax.axis_size("space")
    me = lax.axis_index("member")
    pieces = [shard] + [
        lax.ppermute(shard, "member", ring(members, members - step)) for step in range(1, members)
    ]
    stack = jnp.stack(pieces)
    whole = lax.dynamic_slice_in_dim(jnp.concatenate([stack, stack]), members - me, members, 0)
    bit = 1
    whole = whole[:, None]
    while bit < spaces:
        other = lax.ppermute(whole, "space", flip(spaces, bit))
        mine = (lax.axis_index("space") // bit) % 2
        low = jnp.where(mine == 0, whole, other)
        high = jnp.where(mine == 0, other, whole)
        whole = jnp.concatenate([low, high], axis=1)
        bit *= 2
    return whole


def sum_all(array):
    members = lax.axis_size("member")
    spaces = lax.axis_size("space")
    for axis, count in (("space", spaces), ("member", members)):
        bit = 1
        while bit < count:
            array = array + lax.ppermute(array, axis, flip(count, bit))
            bit *= 2
    return array


def body(
    latent_state,
    member_noise,
    conv_weight,
    norm_gain,
    weight_in,
    weight_down,
    weight_head,
    target_field,
):
    mem_dev, lat_dev, lon_len, width = member_noise.shape
    out_width = weight_head.shape[1]
    members = lax.axis_size("member")
    spaces = lax.axis_size("space")
    devices = members * spaces
    members_all = mem_dev * members
    points_all = lat_dev * spaces * lon_len
    scale = math.sqrt(members_all * out_width / points_all)
    share = 1.0 / (members_all * (members_all - 1))
    me = lax.axis_index("member")
    place = lax.axis_index("space")
    me_s = me.astype(jnp.int32).reshape(1)
    bits = ((place >> jnp.arange(max(2, spaces.bit_length() - 1))) & 1).astype(jnp.int32)
    gain = norm_gain.reshape(1, width)

    edge = (
        jnp.stack([latent_state[0], latent_state[lat_dev - 1]])[None].astype(F32)
        + jnp.stack([member_noise[:, 0], member_noise[:, lat_dev - 1]], axis=1).astype(F32)
    ).astype(BF16)
    above = lax.ppermute(edge[:, 1:], "space", [(i, i + 1) for i in range(spaces - 1)])
    below = lax.ppermute(edge[:, :1], "space", [(i + 1, i) for i in range(spaces - 1)])
    halves = [(tuple(range(1, lat_dev - 1)), ()), ((0, lat_dev - 1), (above, below))]

    saved, pulled = [], []
    for rows, edges in halves:
        kept, sends = forward(
            me_s, member_noise, latent_state, edges, conv_weight, gain,
            weight_in, weight_down, weight_head, target_field, rows, members,
        )
        saved.append(kept)
        pulled.append(
            [sends[0]]
            + [lax.ppermute(sends[k], "member", ring(members, k)) for k in range(1, members)]
        )
    grads, smalls = [], []
    for half, (rows, edges) in enumerate(halves):
        normed, normal, inv, activ, slope, hidden, attract = saved[half]
        pulls = pair_pull(pulled[half])
        pulls = [pulls[0]] + [
            lax.ppermute(pulls[k], "member", ring(members, members - k))
            for k in range(1, members)
        ]
        grads.append(slopes(me_s, attract, pulls, weight_head, weight_down, slope, scale, share))

    def small_of(half):
        rows, edges = halves[half]
        normed, normal, inv = saved[half][:3]
        return norms(
            grads[half][2], weight_in, normal, inv, gain, member_noise, latent_state, edges, rows
        )

    small = small_of(0)
    keep, send = weights(
        bits,
        [saved[h][3] for h in range(2)],
        [grads[h][1] for h in range(2)],
        devices,
        [grads[h][0] for h in range(2)] + [saved[h][5] for h in range(2)],
    )
    down_mine = add_up(*reduce_blocks(me_s, bits, keep, send))
    keep, send = weights(
        bits, [grads[h][2] for h in range(2)], [saved[h][0] for h in range(2)], devices
    )
    in_mine = add_up(*reduce_blocks(me_s, bits, keep, send))
    small = sum_all(small + small_of(1))
    units = weight_in.shape[0] // devices
    unit_pad = pad_to(units, 16)
    head_rows = -(-out_width // devices)
    head_mine = down_mine[unit_pad : unit_pad + head_rows].astype(BF16)
    head_total = gather_all(head_mine).reshape(-1, width)[:out_width].T.astype(F32)
    return (in_mine[:units], down_mine[:units], head_total, small[9], small[:9])


def solution(mesh):
    return jax.shard_map(
        body,
        mesh=mesh,
        in_specs=(
            P("space", None, None),
            P("member", "space", None, None),
            P(),
            P(),
            P(),
            P(),
            P(),
            P("space", None, None),
        ),
        out_specs=(P(("member", "space"), None), P(("member", "space"), None), P(), P(), P()),
        check_vma=False,
    )
```

```python
import functools
import math

import jax
import jax.numpy as jnp
from jax import lax
from jax.experimental import pallas as pl
from jax.experimental.pallas import tpu as pltpu
from jax.sharding import PartitionSpec as P


F32 = jnp.float32
SMALL = 10
BF16 = jnp.bfloat16
LAST = (((1,), (1,)), ((), ()))
FIRST = (((0,), (0,)), ((), ()))
SMEM = pl.BlockSpec(memory_space=pltpu.SMEM)


def dot(left, right, dims=(((1,), (0,)), ((), ()))):
    return lax.dot_general(left, right, dims, preferred_element_type=F32)


def ring(count, step):
    return [(i, (i + step) % count) for i in range(count)]


def flip(count, bit):
    return [(i, i ^ bit) for i in range(count)]


def size_of(shape, kind):
    return math.prod(shape) * jnp.dtype(kind).itemsize


def call(kernel, ins, outs, scratch, name, micros, scalars=1, room=6):
    kept = sum(size_of(part.shape, part.dtype) for part in scratch)
    moved = sum(size_of(x.shape, x.dtype) for x in ins) + sum(size_of(*out) for out in outs)
    return pl.pallas_call(
        kernel,
        in_specs=[SMEM] * scalars
        + [pl.BlockSpec(memory_space=pltpu.VMEM)] * (len(ins) - scalars),
        out_specs=[pl.BlockSpec(memory_space=pltpu.VMEM)] * len(outs),
        out_shape=[jax.ShapeDtypeStruct(shape, kind) for shape, kind in outs],
        scratch_shapes=scratch,
        compiler_params=pltpu.CompilerParams(vmem_limit_bytes=kept + (room << 20)),
        cost_estimate=pl.CostEstimate(
            flops=int(micros * 1e9), bytes_accessed=moved, transcendentals=0
        ),
        name=name,
    )(*ins)


def tile_of(total):
    return next(t for t in range(640, 0, -128) if total % t == 0)


def mixed_row(noise, latent, edges, m, i):
    if i < 0:
        return edges[0][m, 0]
    if i >= latent.shape[0]:
        return edges[1][m, 0]
    return (latent[i].astype(F32) + noise[m, i].astype(F32)).astype(BF16)


def forward_kernel(rows, members, members_all, edged, *refs):
    me_ref, noise, latent = refs[:3]
    edges = refs[3:5] if edged else ()
    conv_w, gain, w_in, w_down, w_head, target = refs[3 + len(edges) : 9 + len(edges)]
    rest = refs[9 + len(edges) :]
    normed, normal, inv, activ, slope, hidden, attract = rest[:7]
    sends = rest[7 : 7 + members]
    mix_s, acc, pred = rest[7 + members :]
    mem_dev, _, lon, width = noise.shape
    span = len(rows) * lon
    tile = tile_of(w_in.shape[0])
    me = me_ref[0]

    def conv_step(m, carry):
        for at, i in enumerate(rows):
            start = pl.multiple_of(m * span + at * lon, lon)
            here = pl.ds(start, lon)
            sums = [None] * 3
            for a in range(3):
                row_b = mixed_row(noise, latent, edges, m, i + a - 1)
                if a == 1:
                    mix_s[here, :] = row_b
                row = row_b.astype(F32)
                for b in range(3):
                    k = 3 * a + b
                    term = conv_w[k : k + 1, :] * row
                    sums[b] = term if sums[b] is None else sums[b] + term
            conv = (
                sums[1] + pltpu.roll(sums[0], 1, axis=0) + pltpu.roll(sums[2], lon - 1, axis=0)
            )
            center = conv - jnp.mean(conv, axis=-1, keepdims=True)
            scale = lax.rsqrt(jnp.mean(center * center, axis=-1, keepdims=True) + 1e-05)
            unit = center * scale
            normal[here, :] = unit
            inv[here, :] = jnp.broadcast_to(scale, (lon, 128))
            normed[here, :] = (unit * gain[...]).astype(BF16)
        return carry

    lax.fori_loop(0, mem_dev, conv_step, 0)
    acc[...] = jnp.zeros(acc.shape, F32)

    def unit_step(t, carry):
        at = pl.ds(pl.multiple_of(t * tile, tile), tile)
        x = dot(normed[...], w_in[at, :], LAST)
        rate = math.sqrt(2.0 / math.pi)
        square = x * x
        tanh = jnp.tanh(rate * x * (1.0 + 0.044715 * square))
        cdf = 0.5 + 0.5 * tanh
        act = (x * cdf).astype(BF16)
        activ[:, at] = act
        slope[:, at] = (
            cdf + 0.5 * x * (1.0 - tanh * tanh) * (rate * (1.0 + (3 * 0.044715) * square))
        ).astype(BF16)
        acc[...] += dot(act, w_down[at, :])
        return carry

    lax.fori_loop(0, w_in.shape[0] // tile, unit_step, 0)
    hid = (mix_s[...].astype(F32) + acc[...]).astype(BF16)
    hidden[...] = hid
    pred[...] = dot(hid, w_head[...], LAST)
    for m in range(mem_dev):
        for at, i in enumerate(rows):
            here = pl.ds(m * span + at * lon, lon)
            error = pred[here, :] - target[i].T
            dist = lax.rsqrt(jnp.sum(error * error, axis=-1, keepdims=True) + 1.0)
            attract[here, :] = error * dist * (1.0 / members_all)
    points = span // members
    for k in range(members):
        chunk = lax.rem(me + k, members)
        for m in range(mem_dev):
            at = pl.ds(pl.multiple_of(m * span + chunk * points, points), points)
            sends[k][m] = pred[at, :].astype(BF16)


def forward(me, noise, latent, edges, conv_w, gain, w_in, w_down, w_head, target, rows, members):
    mem_dev, _, lon, width = noise.shape
    out_width = w_head.shape[0]
    units = w_in.shape[0]
    total = mem_dev * len(rows) * lon
    points = len(rows) * lon // members
    ins = [me, noise, latent, *edges, conv_w, gain, w_in, w_down, w_head, target]
    outs = [
        ((total, width), BF16),
        ((total, width), F32),
        ((total, 128), F32),
        ((total, units), BF16),
        ((total, units), BF16),
        ((total, width), BF16),
        ((total, out_width), F32),
    ] + [((mem_dev, points, out_width), BF16)] * members
    scratch = [
        pltpu.VMEM((total, width), BF16),
        pltpu.VMEM((total, width), F32),
        pltpu.VMEM((total, out_width), F32),
    ]
    kernel = functools.partial(
        forward_kernel, rows, members, members * mem_dev, len(edges) > 0
    )
    out = call(kernel, ins, outs, scratch, "forward", 9)
    return out[:7], out[7:]


def pair_kernel(*refs):
    half = len(refs) // 2
    ins, outs = refs[:half], refs[half:]
    per, points = ins[0].shape[:2]
    step = 16 if points % 16 == 0 else points

    def run(t, carry):
        at = pl.ds(pl.multiple_of(t * step, step), step)
        values = [ref[m, at, :].astype(F32) for ref in ins for m in range(per)]
        pulls = [None] * len(values)
        for a in range(len(values)):
            for b in range(a + 1, len(values)):
                gap = values[a] - values[b]
                pull = gap * lax.rsqrt(jnp.sum(gap * gap, axis=-1, keepdims=True) + 1.0)
                pulls[a] = pull if pulls[a] is None else pulls[a] + pull
                pulls[b] = -pull if pulls[b] is None else pulls[b] - pull
        for index, pull in enumerate(pulls):
            outs[index // per][index % per, at, :] = pull.astype(BF16)
        return carry

    lax.fori_loop(0, points // step, run, 0)


def pair_pull(groups):
    return call(pair_kernel, groups, [(groups[0].shape, BF16)] * len(groups), [], "pair", 2, 0)


def slope_kernel(members, scale, share, *refs):
    me_ref, attract = refs[:2]
    pulls = refs[2 : 2 + members]
    w_head, w_down, slope, grad, ghid, gpre = refs[2 + members :]
    mem_dev, points, _ = pulls[0].shape
    span = attract.shape[0] // mem_dev
    tile = tile_of(w_down.shape[0])
    me = me_ref[0]
    for k in range(members):
        chunk = lax.rem(me + k, members)
        for m in range(mem_dev):
            at = pl.ds(pl.multiple_of(m * span + chunk * points, points), points)
            grad[at, :] = (scale * (attract[at, :] - pulls[k][m].astype(F32) * share)).astype(BF16)
    ghid[...] = dot(grad[...], w_head[...]).astype(BF16)

    def unit_step(t, carry):
        at = pl.ds(pl.multiple_of(t * tile, tile), tile)
        back = dot(ghid[...], w_down[at, :], LAST)
        gpre[:, at] = (slope[:, at].astype(F32) * back).astype(BF16)
        return carry

    lax.fori_loop(0, w_down.shape[0] // tile, unit_step, 0)


def slopes(me, attract, pulls, w_head, w_down, slope, scale, share):
    total, out_width = attract.shape
    outs = [
        ((total, out_width), BF16),
        ((total, w_head.shape[1]), BF16),
        (slope.shape, BF16),
    ]
    kernel = functools.partial(slope_kernel, len(pulls), scale, share)
    ins = [me, attract, *pulls, w_head, w_down, slope]
    return call(kernel, ins, outs, [], "slopes", 3)


def norm_kernel(rows, edged, *refs):
    gpre, w_in, normal, inv, gain, noise, latent = refs[:7]
    edges = refs[7:9] if edged else ()
    small, acc = refs[7 + len(edges) :]
    mem_dev, _, lon, width = noise.shape
    span = len(rows) * lon
    tile = tile_of(w_in.shape[0])
    acc[...] = jnp.zeros(acc.shape, F32)

    def unit_step(t, carry):
        at = pl.ds(pl.multiple_of(t * tile, tile), tile)
        acc[...] += dot(gpre[:, at], w_in[at, :])
        return carry

    lax.fori_loop(0, w_in.shape[0] // tile, unit_step, 0)
    small[...] = jnp.zeros(small.shape, F32)

    def conv_step(m, carry):
        for at, i in enumerate(rows):
            here = pl.ds(pl.multiple_of(m * span + at * lon, lon), lon)
            back = acc[here, :]
            unit = normal[here, :]
            product = back * unit
            small[9:10, :] += jnp.sum(product, axis=0, keepdims=True)
            g = back * gain[...]
            mean = jnp.mean(g, axis=-1, keepdims=True)
            along = jnp.mean(product * gain[...], axis=-1, keepdims=True)
            out = (g - mean - unit * along) * inv[here, 0:1]
            turned = [pltpu.roll(out, lon - 1, axis=0), out, pltpu.roll(out, 1, axis=0)]
            for a in range(3):
                row = mixed_row(noise, latent, edges, m, i + a - 1).astype(F32)
                for b in range(3):
                    k = 3 * a + b
                    small[k : k + 1, :] += jnp.sum(row * turned[b], axis=0, keepdims=True)
        return carry

    lax.fori_loop(0, mem_dev, conv_step, 0)


def norms(gpre, w_in, normal, inv, gain, noise, latent, edges, rows):
    width = w_in.shape[1]
    ins = [gpre, w_in, normal, inv, gain, noise, latent, *edges]
    kernel = functools.partial(norm_kernel, rows, len(edges) > 0)
    scratch = [pltpu.VMEM(normal.shape, F32)]
    return call(kernel, ins, [((16, width), F32)], scratch, "norms", 5, 0)[0]


def emit(source, low, keep, send, j, per):
    rows = keep.shape[1]
    even = source[2 * j * per : 2 * j * per + rows, :]
    odd = source[(2 * j + 1) * per : (2 * j + 1) * per + rows, :]
    keep[j] = jnp.where(low, even, odd)
    send[j] = jnp.where(low, odd, even).astype(BF16)


def weight_kernel(units, info_ref, left_a, left_b, right_a, right_b, keep, send, acc):
    size = left_a.shape[1]
    tile = tile_of(size)
    low = info_ref[1] == 0
    acc[size:, :] = jnp.zeros((acc.shape[0] - size, acc.shape[1]), F32)
    done = 0
    for t in range(size // tile):
        at = pl.ds(t * tile, tile)
        acc[at, :] = dot(left_a[:, at], right_a[...], FIRST) + dot(
            left_b[:, at], right_b[...], FIRST
        )
        while done < keep.shape[0] and (
            t == size // tile - 1 or (2 * done + 1) * units + keep.shape[1] <= (t + 1) * tile
        ):
            emit(acc, low, keep, send, done, units)
            done += 1


def pad_to(value, unit):
    return -(-value // unit) * unit


def weights(info, left, right, devices):
    size = left[0].shape[1]
    width = right[0].shape[1]
    units = size // devices
    rows = pad_to(units, 16)
    scratch = [pltpu.VMEM((pad_to(size + rows - units, 8) + 8, width), F32)]
    outs = [((devices // 2, rows, width), F32), ((devices // 2, rows, width), BF16)]
    kernel = functools.partial(weight_kernel, units)
    return call(kernel, [info, *left, *right], outs, scratch, "weights", 6)


def head_kernel(head_rows, info_ref, *refs):
    grads, hids, smalls = refs[0:2], refs[2:4], refs[4:6]
    keep, send, plain, head = refs[6:]
    wide = grads[0].shape[1]
    plain[0:wide, :] = dot(grads[0][...], hids[0][...], FIRST) + dot(
        grads[1][...], hids[1][...], FIRST
    )
    small = smalls[0][...] + smalls[1][...]
    head[...] = jnp.zeros(head.shape, F32)
    slot = keep.shape[1]
    for block in range(head.shape[0] // slot):
        rows = min(head_rows, max(0, wide - block * head_rows))
        if rows:
            head[block * slot : block * slot + rows, :] = plain[
                block * head_rows : block * head_rows + rows, :
            ]
        if block < SMALL:
            at = block * slot + head_rows
            head[at : at + 1, :] = small[block : block + 1, :]
    low = info_ref[1] == 0
    for j in range(keep.shape[0]):
        emit(head, low, keep, send, j, slot)


def heads(info, grads, hids, smalls, devices):
    wide = grads[0].shape[1]
    width = hids[0].shape[1]
    head_rows = -(-wide // devices)
    slot = pad_to(head_rows + 1, 16)
    scratch = [pltpu.VMEM((wide, width), F32), pltpu.VMEM((devices * slot, width), F32)]
    outs = [((devices // 2, slot, width), F32), ((devices // 2, slot, width), BF16)]
    kernel = functools.partial(head_kernel, head_rows)
    return call(kernel, [info, *grads, *hids, *smalls], outs, scratch, "heads", 2)


def insert(index, place, bit):
    low = (1 << place) - 1
    return ((index >> place) << (place + 1)) | (bit << place) | (index & low)


def merge_kernel(plans, shared, info_ref, *refs):
    count = len(plans)
    given = 1 if shared else count
    keeps, gots = refs[:given], refs[given : 2 * given]
    outs = refs[2 * given :]
    if shared:
        keeps, gots = keeps * count, gots * count
    for flow, (first, rows, place, which) in enumerate(plans):
        bit = info_ref[1 + which]
        keep, got = keeps[flow], gots[flow]
        out_keep, out_send = outs[2 * flow : 2 * flow + 2]
        at = pl.ds(first, rows)

        def step(i, carry, keep=keep, got=got, out_keep=out_keep, out_send=out_send, at=at, place=place, bit=bit):
            mine = insert(i, place, bit)
            other = insert(i, place, 1 - bit)
            out_keep[i] = keep[mine, at, :] + got[mine, at, :].astype(F32)
            out_send[i] = (keep[other, at, :] + got[other, at, :].astype(F32)).astype(BF16)
            return carry

        lax.fori_loop(0, out_keep.shape[0], step, 0)


def merge(info, keeps, gots, plans):
    width = keeps[0].shape[2]
    outs = []
    for keep, (_, rows, _, _) in zip(keeps, plans):
        blocks = keep.shape[0] // 2
        outs += [((blocks, rows, width), F32), ((blocks, rows, width), BF16)]
    shared = keeps[0] is keeps[-1]
    kernel = functools.partial(merge_kernel, plans, shared)
    if shared:
        keeps, gots = keeps[:1], gots[:1]
    out = call(kernel, [info, *keeps, *gots], outs, [], "merge", 1)
    return out[0::2], out[1::2]


def turn_kernel(members, firsts, info_ref, *refs):
    count = len(firsts)
    keeps, gots = refs[:count], refs[count : 2 * count]
    outs = refs[2 * count :]
    for k in range(members):
        block = lax.rem(info_ref[0] + k, members)
        for flow, first in enumerate(firsts):
            value = keeps[flow][block] + gots[flow][block].astype(F32)
            outs[k][first : first + value.shape[0], :] = value.astype(outs[k].dtype)


def turn(info, keeps, gots, members):
    width = keeps[0].shape[2]
    firsts, rows = [], 0
    for keep in keeps:
        firsts.append(rows)
        rows += keep.shape[1]
    outs = [((rows, width), F32)] + [((rows, width), BF16)] * (members - 1)
    kernel = functools.partial(turn_kernel, members, tuple(firsts))
    return call(kernel, [info, *keeps, *gots], outs, [], "turn", 1)


def start_blocks(send):
    return lax.ppermute(send, "space", flip(lax.axis_size("space"), 1))


def flows_of(rows):
    levels = list(range(1, lax.axis_size("space").bit_length() - 1))
    cut = pad_to(rows, 32) // 2
    flows = [(0, cut, levels)]
    if rows > cut:
        flows.append((cut, rows - cut, levels[::-1]))
    return flows


def merge_blocks(info, keeps, gots, flows, depth):
    spaces = lax.axis_size("space")
    plans = []
    for first, size, order in flows:
        place = sum(1 for other in order[depth:] if other < order[depth])
        plans.append((first if depth == 0 else 0, size, place, order[depth]))
    keeps, sends = merge(info, keeps, gots, tuple(plans))
    gots = [
        lax.ppermute(part, "space", flip(spaces, 1 << order[depth]))
        for part, (_, _, order) in zip(sends, flows)
    ]
    return list(keeps), list(gots)


def turn_blocks(info, keeps, gots):
    members = lax.axis_size("member")
    parts = turn(info, keeps, gots, members)
    return parts[0], [
        lax.ppermute(parts[k], "member", ring(members, k)) for k in range(1, members)
    ]


def add_up(own, others):
    for other in others:
        own = own + other.astype(F32)
    return own


def round_kernel(info_ref, keep, got, own):
    own[...] = (keep[...] + got[...].astype(F32)).astype(BF16)


def fold_kernel(info_ref, *refs):
    pieces, out, hold = refs[:-2], refs[-2], refs[-1]
    members = len(pieces)
    for k in range(members):
        hold[k] = pieces[k][...].astype(F32)
    total = hold[info_ref[0]]
    for m in range(1, members):
        total = total + hold[lax.rem(info_ref[0] + members - m, members)]
    out[...] = total.astype(BF16)


def turned(index, count):
    bits = count.bit_length() - 1
    return sum(((index >> b) & 1) << (bits - 1 - b) for b in range(bits))


def place_kernel(info_ref, rel, out):
    spaces, members = rel.shape[:2]
    place = 0
    for bit in range(spaces.bit_length() - 1):
        place = place + info_ref[1 + bit] * (1 << bit)
    for r in range(spaces):
        for m in range(members):
            out[m * spaces + (place ^ turned(r, spaces))] = rel[r, m].astype(F32)


def fold_members(info, keep, got):
    members = lax.axis_size("member")
    own = call(round_kernel, [info, keep, got], [(keep.shape, BF16)], [], "round", 1)[0]
    return own, [lax.ppermute(own, "member", ring(members, k)) for k in range(1, members)]


def fold(info, pieces):
    scratch = [pltpu.VMEM((len(pieces),) + pieces[0].shape, F32)]
    return call(fold_kernel, [info, *pieces], [(pieces[0].shape, BF16)], scratch, "fold", 1)[0]


def spread_step(whole, bit):
    other = lax.ppermute(whole, "space", flip(lax.axis_size("space"), bit))
    return jnp.concatenate([whole, other], axis=0)


def placed(info, whole):
    spaces, members = whole.shape[:2]
    outs = [((members * spaces,) + whole.shape[2:], F32)]
    return call(place_kernel, [info, whole], outs, [], "place", 1)[0]


def after(value, other):
    return lax.optimization_barrier((value, other))


def edge_kernel(info_ref, latent, noise, first, last):
    for row, out in ((0, first), (latent.shape[0] - 1, last)):
        for m in range(noise.shape[0]):
            out[m, 0] = (latent[row].astype(F32) + noise[m, row].astype(F32)).astype(BF16)


def edge_rows(info, latent, noise):
    mem_dev, _, lon, width = noise.shape
    outs = [((mem_dev, 1, lon, width), BF16)] * 2
    return call(edge_kernel, [info, latent, noise], outs, [], "edges", 1)


def body(
    latent_state,
    member_noise,
    conv_weight,
    norm_gain,
    weight_in,
    weight_down,
    weight_head,
    target_field,
):
    mem_dev, lat_dev, lon_len, width = member_noise.shape
    out_width = weight_head.shape[1]
    members = lax.axis_size("member")
    spaces = lax.axis_size("space")
    devices = members * spaces
    members_all = mem_dev * members
    points_all = lat_dev * spaces * lon_len
    scale = math.sqrt(members_all * out_width / points_all)
    share = 1.0 / (members_all * (members_all - 1))
    place = lax.axis_index("space")
    info = jnp.stack(
        [lax.axis_index("member")] + [(place >> b) & 1 for b in range(spaces.bit_length() - 1)]
    ).astype(jnp.int32)
    gain = norm_gain.reshape(1, width)
    head_t = weight_head.T
    target_t = target_field.transpose(0, 2, 1)

    first, last = edge_rows(info, latent_state, member_noise)
    above = lax.ppermute(last, "space", [(i, i + 1) for i in range(spaces - 1)])
    below = lax.ppermute(first, "space", [(i + 1, i) for i in range(spaces - 1)])
    halves = [(tuple(range(1, lat_dev - 1)), ()), ((0, lat_dev - 1), (above, below))]

    saved, pulled = [], []
    for rows, edges in halves:
        kept, sends = forward(
            info, member_noise, latent_state, edges, conv_weight, gain,
            weight_in, weight_down, head_t, target_t, rows, members,
        )
        saved.append(kept)
        pulled.append(
            [sends[0]]
            + [lax.ppermute(sends[k], "member", ring(members, k)) for k in range(1, members)]
        )
    pulled[0][-1], pulled[1][0] = lax.optimization_barrier((pulled[0][-1], pulled[1][0]))
    backs = []
    for half in range(2):
        pulls = pair_pull(pulled[half])
        backs.append(
            [pulls[0]]
            + [
                lax.ppermute(pulls[k], "member", ring(members, members - k))
                for k in range(1, members)
            ]
        )
    backs[0][0], backs[1][0] = lax.optimization_barrier((backs[0][0], backs[1][0]))
    grads, smalls = [], []
    for half, (rows, edges) in enumerate(halves):
        normed, normal, inv, activ, slope, hidden, attract = saved[half]
        if half:
            attract, smalls[0] = lax.optimization_barrier((attract, smalls[0]))
        grads.append(
            slopes(info, attract, backs[half], head_t, weight_down, slope, scale, share)
        )
        smalls.append(
            norms(
                grads[half][2], weight_in, normal, inv, gain, member_noise, latent_state,
                edges, rows,
            )
        )

    hids = [saved[h][5] for h in range(2)]
    keep_h, send_h = heads(info, [grads[h][0] for h in range(2)], hids, smalls, devices)
    got_h = start_blocks(send_h)
    keep_d, send_d = weights(
        info, [saved[h][3] for h in range(2)], [grads[h][1] for h in range(2)], devices
    )
    got_d = start_blocks(send_d)
    flows_h, flows_d = flows_of(keep_h.shape[1]), flows_of(keep_d.shape[1])
    keep_h, keep_d = after(keep_h, keep_d)
    part_h = merge_blocks(info, [keep_h], [got_h], flows_h, 0)
    gpre = [grads[h][2] for h in range(2)]
    gpre[1], part_h[0][0] = after(gpre[1], part_h[0][0])
    keep_i, send_i = weights(info, gpre, [saved[h][0] for h in range(2)], devices)
    got_i = start_blocks(send_i)
    keep_d, keep_i = after(keep_d, keep_i)
    part_d = [keep_d] * len(flows_d), [got_d] * len(flows_d)
    part_d = merge_blocks(info, *part_d, flows_d, 0)
    depths = spaces.bit_length() - 2
    part_h[0][0], part_d[0][0] = after(part_h[0][0], part_d[0][0])
    for depth in range(1, depths):
        part_h = merge_blocks(info, *part_h, flows_h, depth)
    keep_i, part_h[0][0] = after(keep_i, part_h[0][0])
    part_i = [keep_i] * len(flows_d), [got_i] * len(flows_d)
    part_i = merge_blocks(info, *part_i, flows_d, 0)
    part_h[0][0], part_i[0][0] = after(part_h[0][0], part_i[0][0])
    own_h, others_h = fold_members(info, part_h[0][0], part_h[1][0])
    part_d[0][0], own_h = after(part_d[0][0], own_h)
    for depth in range(1, depths):
        part_d = merge_blocks(info, *part_d, flows_d, depth)
        part_i[0][0], part_d[0][0] = after(part_i[0][0], part_d[0][0])
        part_i = merge_blocks(info, *part_i, flows_d, depth)
        part_d[0][0], part_i[0][0] = after(part_d[0][0], part_i[0][0])
    own_h, part_i[0][0] = after(own_h, part_i[0][0])
    whole = fold(info, [own_h, *others_h])[None]
    bit = spaces // 2
    whole = spread_step(whole, bit)
    own_d, others_d = turn_blocks(info, *part_d)
    part_i[0][0], own_d = after(part_i[0][0], own_d)
    own_i, others_i = turn_blocks(info, *part_i)
    whole, own_i = after(whole, own_i)
    while bit > 1:
        bit //= 2
        whole = spread_step(whole, bit)
    gathered = placed(info, whole)
    units = weight_in.shape[0] // devices
    head_rows = -(-out_width // devices)
    head_total = gathered[:, :head_rows].reshape(-1, width)[:out_width].T
    small = gathered[:SMALL, head_rows]
    in_mine = add_up(own_i, others_i)[:units]
    down_mine = add_up(own_d, others_d)[:units]
    return (in_mine, down_mine, head_total, small[9], small[:9])


def solution(mesh):
    return jax.shard_map(
        body,
        mesh=mesh,
        in_specs=(
            P("space", None, None),
            P("member", "space", None, None),
            P(),
            P(),
            P(),
            P(),
            P(),
            P("space", None, None),
        ),
        out_specs=(P(("member", "space"), None), P(("member", "space"), None), P(), P(), P()),
        check_vma=False,
    )
```

```python
import functools
import math

import jax
import jax.numpy as jnp
from jax import lax
from jax.experimental import pallas as pl
from jax.experimental.pallas import tpu as pltpu
from jax.sharding import PartitionSpec as P


F32 = jnp.float32
SMALL = 10
BF16 = jnp.bfloat16
LAST = (((1,), (1,)), ((), ()))
FIRST = (((0,), (0,)), ((), ()))
SMEM = pl.BlockSpec(memory_space=pltpu.SMEM)


def dot(left, right, dims=(((1,), (0,)), ((), ()))):
    return lax.dot_general(left, right, dims, preferred_element_type=F32)


def ring(count, step):
    return [(i, (i + step) % count) for i in range(count)]


def flip(count, bit):
    return [(i, i ^ bit) for i in range(count)]


def size_of(shape, kind):
    return math.prod(shape) * jnp.dtype(kind).itemsize


def call(kernel, ins, outs, scratch, micros, scalars=1, room=6):
    kept = sum(size_of(part.shape, part.dtype) for part in scratch)
    moved = sum(size_of(x.shape, x.dtype) for x in ins) + sum(size_of(*out) for out in outs)
    return pl.pallas_call(
        kernel,
        in_specs=[SMEM] * scalars
        + [pl.BlockSpec(memory_space=pltpu.VMEM)] * (len(ins) - scalars),
        out_specs=[pl.BlockSpec(memory_space=pltpu.VMEM)] * len(outs),
        out_shape=[jax.ShapeDtypeStruct(shape, kind) for shape, kind in outs],
        scratch_shapes=scratch,
        compiler_params=pltpu.CompilerParams(vmem_limit_bytes=kept + (room << 20)),
        cost_estimate=pl.CostEstimate(
            flops=int(micros * 1e9), bytes_accessed=moved, transcendentals=0
        ),
    )(*ins)


def tile_of(total):
    return next(t for t in range(640, 0, -128) if total % t == 0)


def mixed_row(mixed, edges, m, i):
    if i < 0:
        return edges[0][m, 0]
    if i >= mixed.shape[1]:
        return edges[1][m, 0]
    return mixed[m, i]


def forward_kernel(rows, members, members_all, edged, *refs):
    me_ref, mixed = refs[:2]
    edges = refs[2:4] if edged else ()
    conv_w, gain, w_in, w_down, w_head, target = refs[2 + len(edges) : 8 + len(edges)]
    rest = refs[8 + len(edges) :]
    normed, normal, inv, activ, slope, hidden, attract = rest[:7]
    sends = rest[7 : 7 + members]
    mix_s, pred = rest[7 + members :]
    mem_dev, _, lon, _ = mixed.shape
    span = len(rows) * lon
    tile = tile_of(w_in.shape[0])
    me = me_ref[0]

    def conv_step(m, carry):
        for at, i in enumerate(rows):
            start = pl.multiple_of(m * span + at * lon, lon)
            here = pl.ds(start, lon)
            sums = [None] * 3
            for a in range(3):
                row_b = mixed_row(mixed, edges, m, i + a - 1)
                if a == 1:
                    mix_s[here, :] = row_b
                row = row_b.astype(F32)
                for b in range(3):
                    k = 3 * a + b
                    term = conv_w[k : k + 1, :] * row
                    sums[b] = term if sums[b] is None else sums[b] + term
            conv = (
                sums[1] + pltpu.roll(sums[0], 1, axis=0) + pltpu.roll(sums[2], lon - 1, axis=0)
            )
            center = conv - jnp.mean(conv, axis=-1, keepdims=True)
            scale = lax.rsqrt(jnp.mean(center * center, axis=-1, keepdims=True) + 1e-05)
            unit = center * scale
            normal[here, :] = unit
            inv[here, :] = jnp.broadcast_to(scale, (lon, 128))
            normed[here, :] = (unit * gain[...]).astype(BF16)
        return carry

    lax.fori_loop(0, mem_dev, conv_step, 0)
    rate = math.sqrt(2.0 / math.pi)
    for t in range(w_in.shape[0] // tile):
        at = pl.ds(t * tile, tile)
        x = dot(normed[...], w_in[at, :], LAST)
        linear = rate * x
        bend = 1.0 + 0.044715 * (x * x)
        tanh = jnp.tanh(linear * bend)
        half = 0.5 + 0.5 * tanh
        activ[:, at] = (x * half).astype(BF16)
        slope[:, at] = (
            half * (1.0 + (1.0 - tanh) * (linear * (3.0 * bend - 2.0)))
        ).astype(BF16)
    hid = (mix_s[...].astype(F32) + dot(activ[...], w_down[...])).astype(BF16)
    hidden[...] = hid
    pred[...] = dot(hid, w_head[...], LAST)
    for m in range(mem_dev):
        for at, i in enumerate(rows):
            here = pl.ds(m * span + at * lon, lon)
            error = pred[here, :] - target[i].T
            dist = lax.rsqrt(jnp.sum(error * error, axis=-1, keepdims=True) + 1.0)
            attract[here, :] = error * dist * (1.0 / members_all)
    points = span // members
    for k in range(members):
        chunk = lax.rem(me + k, members)
        for m in range(mem_dev):
            at = pl.ds(pl.multiple_of(m * span + chunk * points, points), points)
            sends[k][m] = pred[at, :].astype(BF16)


def forward(me, mixed, edges, conv_w, gain, w_in, w_down, w_head, target, rows, members):
    mem_dev, _, lon, width = mixed.shape
    out_width = w_head.shape[0]
    units = w_in.shape[0]
    total = mem_dev * len(rows) * lon
    points = len(rows) * lon // members
    ins = [me, mixed, *edges, conv_w, gain, w_in, w_down, w_head, target]
    outs = [
        ((total, width), BF16),
        ((total, width), F32),
        ((total, 128), F32),
        ((total, units), BF16),
        ((total, units), BF16),
        ((total, width), BF16),
        ((total, out_width), F32),
    ] + [((mem_dev, points, out_width), BF16)] * members
    scratch = [
        pltpu.VMEM((total, width), BF16),
        pltpu.VMEM((total, out_width), F32),
    ]
    kernel = functools.partial(
        forward_kernel, rows, members, members * mem_dev, len(edges) > 0
    )
    out = call(kernel, ins, outs, scratch, 9)
    return out[:7], out[7:]


def pair_kernel(*refs):
    half = len(refs) // 2
    ins, outs = refs[:half], refs[half:]
    per, points = ins[0].shape[:2]
    step = 16 if points % 16 == 0 else points

    def run(t, carry):
        at = pl.ds(pl.multiple_of(t * step, step), step)
        values = [ref[m, at, :].astype(F32) for ref in ins for m in range(per)]
        pulls = [None] * len(values)
        for a in range(len(values)):
            for b in range(a + 1, len(values)):
                gap = values[a] - values[b]
                pull = gap * lax.rsqrt(jnp.sum(gap * gap, axis=-1, keepdims=True) + 1.0)
                pulls[a] = pull if pulls[a] is None else pulls[a] + pull
                pulls[b] = -pull if pulls[b] is None else pulls[b] - pull
        for index, pull in enumerate(pulls):
            outs[index // per][index % per, at, :] = pull.astype(BF16)
        return carry

    lax.fori_loop(0, points // step, run, 0)


def pair_pull(groups):
    return call(pair_kernel, groups, [(groups[0].shape, BF16)] * len(groups), [], 2, 0)


def slope_kernel(members, scale, share, *refs):
    me_ref, attract = refs[:2]
    pulls = refs[2 : 2 + members]
    w_head, w_down, slope, grad, ghid, gpre = refs[2 + members :]
    mem_dev, points, _ = pulls[0].shape
    span = attract.shape[0] // mem_dev
    tile = tile_of(w_down.shape[0])
    me = me_ref[0]
    for k in range(members):
        chunk = lax.rem(me + k, members)
        for m in range(mem_dev):
            at = pl.ds(pl.multiple_of(m * span + chunk * points, points), points)
            grad[at, :] = (scale * (attract[at, :] - pulls[k][m].astype(F32) * share)).astype(BF16)
    ghid[...] = dot(grad[...], w_head[...]).astype(BF16)

    def unit_step(t, carry):
        at = pl.ds(pl.multiple_of(t * tile, tile), tile)
        back = dot(ghid[...], w_down[at, :], LAST)
        gpre[:, at] = (slope[:, at].astype(F32) * back).astype(BF16)
        return carry

    lax.fori_loop(0, w_down.shape[0] // tile, unit_step, 0)


def slopes(me, attract, pulls, w_head, w_down, slope, scale, share):
    total, out_width = attract.shape
    outs = [
        ((total, out_width), BF16),
        ((total, w_head.shape[1]), BF16),
        (slope.shape, BF16),
    ]
    kernel = functools.partial(slope_kernel, len(pulls), scale, share)
    ins = [me, attract, *pulls, w_head, w_down, slope]
    return call(kernel, ins, outs, [], 3)


def norm_kernel(rows, edged, *refs):
    gpre, w_in, normal, inv, gain, mixed = refs[:6]
    edges = refs[6:8] if edged else ()
    small, acc = refs[6 + len(edges) :]
    mem_dev, _, lon, _ = mixed.shape
    span = len(rows) * lon
    acc[...] = dot(gpre[...], w_in[...])
    small[...] = jnp.zeros(small.shape, F32)

    def conv_step(m, carry):
        for at, i in enumerate(rows):
            here = pl.ds(pl.multiple_of(m * span + at * lon, lon), lon)
            back = acc[here, :]
            unit = normal[here, :]
            product = back * unit
            small[9:10, :] += jnp.sum(product, axis=0, keepdims=True)
            g = back * gain[...]
            mean = jnp.mean(g, axis=-1, keepdims=True)
            along = jnp.mean(product * gain[...], axis=-1, keepdims=True)
            out = (g - mean - unit * along) * inv[here, 0:1]
            turned = [pltpu.roll(out, lon - 1, axis=0), out, pltpu.roll(out, 1, axis=0)]
            for a in range(3):
                row = mixed_row(mixed, edges, m, i + a - 1).astype(F32)
                for b in range(3):
                    k = 3 * a + b
                    small[k : k + 1, :] += jnp.sum(row * turned[b], axis=0, keepdims=True)
        return carry

    lax.fori_loop(0, mem_dev, conv_step, 0)


def norms(gpre, w_in, normal, inv, gain, mixed, edges, rows):
    width = w_in.shape[1]
    ins = [gpre, w_in, normal, inv, gain, mixed, *edges]
    kernel = functools.partial(norm_kernel, rows, len(edges) > 0)
    scratch = [pltpu.VMEM(normal.shape, F32)]
    return call(kernel, ins, [((16, width), F32)], scratch, 5, 0)[0]


def emit(source, low, keep, send, j, per):
    rows = keep.shape[1]
    even = source[2 * j * per : 2 * j * per + rows, :]
    odd = source[(2 * j + 1) * per : (2 * j + 1) * per + rows, :]
    keep[j] = jnp.where(low, even, odd)
    send[j] = jnp.where(low, odd, even).astype(BF16)


def weight_kernel(units, info_ref, left_a, left_b, right_a, right_b, keep, send, acc):
    size = left_a.shape[1]
    tile = tile_of(size)
    low = info_ref[1] == 0
    acc[size:, :] = jnp.zeros((acc.shape[0] - size, acc.shape[1]), F32)
    done = 0
    for t in range(size // tile):
        at = pl.ds(t * tile, tile)
        acc[at, :] = dot(left_a[:, at], right_a[...], FIRST) + dot(
            left_b[:, at], right_b[...], FIRST
        )
        while done < keep.shape[0] and (
            t == size // tile - 1 or (2 * done + 1) * units + keep.shape[1] <= (t + 1) * tile
        ):
            emit(acc, low, keep, send, done, units)
            done += 1


def pad_to(value, unit):
    return -(-value // unit) * unit


def weights(info, left, right, devices):
    size = left[0].shape[1]
    width = right[0].shape[1]
    units = size // devices
    rows = pad_to(units, 16)
    scratch = [pltpu.VMEM((pad_to(size + rows - units, 8) + 8, width), F32)]
    outs = [((devices // 2, rows, width), F32), ((devices // 2, rows, width), BF16)]
    kernel = functools.partial(weight_kernel, units)
    return call(kernel, [info, *left, *right], outs, scratch, 6)


def head_kernel(head_rows, info_ref, *refs):
    grads, hids, smalls = refs[0:2], refs[2:4], refs[4:6]
    keep, send, plain, head = refs[6:]
    wide = grads[0].shape[1]
    plain[0:wide, :] = dot(grads[0][...], hids[0][...], FIRST) + dot(
        grads[1][...], hids[1][...], FIRST
    )
    small = smalls[0][...] + smalls[1][...]
    head[...] = jnp.zeros(head.shape, F32)
    slot = keep.shape[1]
    for block in range(head.shape[0] // slot):
        rows = min(head_rows, max(0, wide - block * head_rows))
        if rows:
            head[block * slot : block * slot + rows, :] = plain[
                block * head_rows : block * head_rows + rows, :
            ]
        if block < SMALL:
            at = block * slot + head_rows
            head[at : at + 1, :] = small[block : block + 1, :]
    low = info_ref[1] == 0
    for j in range(keep.shape[0]):
        emit(head, low, keep, send, j, slot)


def heads(info, grads, hids, smalls, devices):
    wide = grads[0].shape[1]
    width = hids[0].shape[1]
    head_rows = -(-wide // devices)
    slot = pad_to(head_rows + 1, 16)
    scratch = [pltpu.VMEM((wide, width), F32), pltpu.VMEM((devices * slot, width), F32)]
    outs = [((devices // 2, slot, width), F32), ((devices // 2, slot, width), BF16)]
    kernel = functools.partial(head_kernel, head_rows)
    return call(kernel, [info, *grads, *hids, *smalls], outs, scratch, 2)


def insert(index, place, bit):
    low = (1 << place) - 1
    return ((index >> place) << (place + 1)) | (bit << place) | (index & low)


def merge_kernel(plans, shared, info_ref, *refs):
    count = len(plans)
    given = 1 if shared else count
    keeps, gots = refs[:given], refs[given : 2 * given]
    outs = refs[2 * given :]
    if shared:
        keeps, gots = keeps * count, gots * count
    for flow, (first, rows, place, which) in enumerate(plans):
        bit = info_ref[1 + which]
        keep, got = keeps[flow], gots[flow]
        out_keep, out_send = outs[2 * flow : 2 * flow + 2]
        at = pl.ds(first, rows)

        def step(i, carry, keep=keep, got=got, out_keep=out_keep, out_send=out_send, at=at, place=place, bit=bit):
            mine = insert(i, place, bit)
            other = insert(i, place, 1 - bit)
            out_keep[i] = keep[mine, at, :] + got[mine, at, :].astype(F32)
            out_send[i] = (keep[other, at, :] + got[other, at, :].astype(F32)).astype(BF16)
            return carry

        lax.fori_loop(0, out_keep.shape[0], step, 0)


def merge(info, keeps, gots, plans):
    width = keeps[0].shape[2]
    outs = []
    for keep, (_, rows, _, _) in zip(keeps, plans):
        blocks = keep.shape[0] // 2
        outs += [((blocks, rows, width), F32), ((blocks, rows, width), BF16)]
    shared = keeps[0] is keeps[-1]
    kernel = functools.partial(merge_kernel, plans, shared)
    if shared:
        keeps, gots = keeps[:1], gots[:1]
    out = call(kernel, [info, *keeps, *gots], outs, [], 1)
    return out[0::2], out[1::2]


def turn_kernel(members, firsts, info_ref, *refs):
    count = len(firsts)
    keeps, gots = refs[:count], refs[count : 2 * count]
    outs = refs[2 * count :]
    for k in range(members):
        block = lax.rem(info_ref[0] + k, members)
        for flow, first in enumerate(firsts):
            value = keeps[flow][block] + gots[flow][block].astype(F32)
            outs[k][first : first + value.shape[0], :] = value.astype(outs[k].dtype)


def turn(info, keeps, gots, members):
    width = keeps[0].shape[2]
    firsts, rows = [], 0
    for keep in keeps:
        firsts.append(rows)
        rows += keep.shape[1]
    outs = [((rows, width), F32)] + [((rows, width), BF16)] * (members - 1)
    kernel = functools.partial(turn_kernel, members, tuple(firsts))
    return call(kernel, [info, *keeps, *gots], outs, [], 1)


def start_blocks(send):
    return lax.ppermute(send, "space", flip(lax.axis_size("space"), 1))


def flows_of(rows):
    levels = list(range(1, lax.axis_size("space").bit_length() - 1))
    cut = pad_to(rows, 32) // 2
    flows = [(0, cut, levels)]
    if rows > cut:
        flows.append((cut, rows - cut, levels[::-1]))
    return flows


def merge_blocks(info, keeps, gots, flows, depth):
    spaces = lax.axis_size("space")
    plans = []
    for first, size, order in flows:
        place = sum(1 for other in order[depth:] if other < order[depth])
        plans.append((first if depth == 0 else 0, size, place, order[depth]))
    keeps, sends = merge(info, keeps, gots, tuple(plans))
    gots = [
        lax.ppermute(part, "space", flip(spaces, 1 << order[depth]))
        for part, (_, _, order) in zip(sends, flows)
    ]
    return list(keeps), list(gots)


def turn_blocks(info, keeps, gots):
    members = lax.axis_size("member")
    parts = turn(info, keeps, gots, members)
    return parts[0], [
        lax.ppermute(parts[k], "member", ring(members, k)) for k in range(1, members)
    ]


def add_up(own, others):
    for other in others:
        own = own + other.astype(F32)
    return own


def round_kernel(info_ref, keep, got, own):
    own[...] = (keep[...] + got[...].astype(F32)).astype(BF16)


def fold_kernel(info_ref, *refs):
    pieces, out, hold = refs[:-2], refs[-2], refs[-1]
    members = len(pieces)
    for k in range(members):
        hold[k] = pieces[k][...].astype(F32)
    total = hold[info_ref[0]]
    for m in range(1, members):
        total = total + hold[lax.rem(info_ref[0] + members - m, members)]
    out[...] = total.astype(BF16)


def turned(index, count):
    bits = count.bit_length() - 1
    return sum(((index >> b) & 1) << (bits - 1 - b) for b in range(bits))


def place_kernel(info_ref, rel, out):
    spaces, members = rel.shape[:2]
    place = 0
    for bit in range(spaces.bit_length() - 1):
        place = place + info_ref[1 + bit] * (1 << bit)
    for r in range(spaces):
        for m in range(members):
            out[m * spaces + (place ^ turned(r, spaces))] = rel[r, m].astype(F32)


def fold_members(info, keep, got):
    members = lax.axis_size("member")
    own = call(round_kernel, [info, keep, got], [(keep.shape, BF16)], [], 1)[0]
    return own, [lax.ppermute(own, "member", ring(members, k)) for k in range(1, members)]


def fold(info, pieces):
    scratch = [pltpu.VMEM((len(pieces),) + pieces[0].shape, F32)]
    return call(fold_kernel, [info, *pieces], [(pieces[0].shape, BF16)], scratch, 1)[0]


def spread_step(whole, bit):
    other = lax.ppermute(whole, "space", flip(lax.axis_size("space"), bit))
    return jnp.concatenate([whole, other], axis=0)


def placed(info, whole):
    spaces, members = whole.shape[:2]
    outs = [((members * spaces,) + whole.shape[2:], F32)]
    return call(place_kernel, [info, whole], outs, [], 1)[0]


def after(value, other):
    return lax.optimization_barrier((value, other))


def mix_kernel(info_ref, latent, noise, mixed, first, last):
    mem_dev, lat = noise.shape[:2]
    for i in range(lat):
        for m in range(mem_dev):
            value = (latent[i].astype(F32) + noise[m, i].astype(F32)).astype(BF16)
            mixed[m, i] = value
            if i == 0:
                first[m, 0] = value
            if i == lat - 1:
                last[m, 0] = value


def mix_rows(info, latent, noise):
    mem_dev, _, lon, width = noise.shape
    edge = ((mem_dev, 1, lon, width), BF16)
    outs = [(noise.shape, BF16), edge, edge]
    return call(mix_kernel, [info, latent, noise], outs, [], 1)


def body(
    latent_state,
    member_noise,
    conv_weight,
    norm_gain,
    weight_in,
    weight_down,
    weight_head,
    target_field,
):
    mem_dev, lat_dev, lon_len, width = member_noise.shape
    out_width = weight_head.shape[1]
    members = lax.axis_size("member")
    spaces = lax.axis_size("space")
    devices = members * spaces
    members_all = mem_dev * members
    points_all = lat_dev * spaces * lon_len
    scale = math.sqrt(members_all * out_width / points_all)
    share = 1.0 / (members_all * (members_all - 1))
    place = lax.axis_index("space")
    info = jnp.stack(
        [lax.axis_index("member")] + [(place >> b) & 1 for b in range(spaces.bit_length() - 1)]
    ).astype(jnp.int32)
    gain = norm_gain.reshape(1, width)
    head_t = weight_head.T
    target_t = target_field.transpose(0, 2, 1)

    mixed, first, last = mix_rows(info, latent_state, member_noise)
    above = lax.ppermute(last, "space", [(i, i + 1) for i in range(spaces - 1)])
    below = lax.ppermute(first, "space", [(i + 1, i) for i in range(spaces - 1)])
    halves = [(tuple(range(1, lat_dev - 1)), ()), ((0, lat_dev - 1), (above, below))]

    saved, pulled = [], []
    for rows, edges in halves:
        kept, sends = forward(
            info, mixed, edges, conv_weight, gain,
            weight_in, weight_down, head_t, target_t, rows, members,
        )
        saved.append(kept)
        pulled.append(
            [sends[0]]
            + [lax.ppermute(sends[k], "member", ring(members, k)) for k in range(1, members)]
        )
    pulled[0][-1], pulled[1][0] = lax.optimization_barrier((pulled[0][-1], pulled[1][0]))
    backs = []
    for half in range(2):
        pulls = pair_pull(pulled[half])
        backs.append(
            [pulls[0]]
            + [
                lax.ppermute(pulls[k], "member", ring(members, members - k))
                for k in range(1, members)
            ]
        )
    backs[0][0], backs[1][0] = lax.optimization_barrier((backs[0][0], backs[1][0]))
    grads, smalls = [], []
    for half, (rows, edges) in enumerate(halves):
        _, normal, inv, _, slope, _, attract = saved[half]
        if half:
            attract, smalls[0] = lax.optimization_barrier((attract, smalls[0]))
        grads.append(
            slopes(info, attract, backs[half], head_t, weight_down, slope, scale, share)
        )
        smalls.append(
            norms(
                grads[half][2], weight_in, normal, inv, gain, mixed, edges, rows,
            )
        )

    hids = [saved[h][5] for h in range(2)]
    keep_h, send_h = heads(info, [grads[h][0] for h in range(2)], hids, smalls, devices)
    got_h = start_blocks(send_h)
    keep_d, send_d = weights(
        info, [saved[h][3] for h in range(2)], [grads[h][1] for h in range(2)], devices
    )
    got_d = start_blocks(send_d)
    flows_h, flows_d = flows_of(keep_h.shape[1]), flows_of(keep_d.shape[1])
    keep_h, keep_d = after(keep_h, keep_d)
    part_h = merge_blocks(info, [keep_h], [got_h], flows_h, 0)
    gpre = [grads[h][2] for h in range(2)]
    gpre[1], part_h[0][0] = after(gpre[1], part_h[0][0])
    keep_i, send_i = weights(info, gpre, [saved[h][0] for h in range(2)], devices)
    got_i = start_blocks(send_i)
    part_h[0][0], keep_i = after(part_h[0][0], keep_i)
    depths = spaces.bit_length() - 2
    for depth in range(1, depths):
        part_h = merge_blocks(info, *part_h, flows_h, depth)
    keep_d, part_h[0][0] = after(keep_d, part_h[0][0])
    part_d = [keep_d] * len(flows_d), [got_d] * len(flows_d)
    part_d = merge_blocks(info, *part_d, flows_d, 0)
    keep_i, part_d[0][0] = after(keep_i, part_d[0][0])
    part_i = [keep_i] * len(flows_d), [got_i] * len(flows_d)
    part_i = merge_blocks(info, *part_i, flows_d, 0)
    part_h[0][0], part_i[0][0] = after(part_h[0][0], part_i[0][0])
    own_h, others_h = fold_members(info, part_h[0][0], part_h[1][0])
    part_d[0][0], own_h = after(part_d[0][0], own_h)
    for depth in range(1, depths):
        part_d = merge_blocks(info, *part_d, flows_d, depth)
        part_i[0][0], part_d[0][0] = after(part_i[0][0], part_d[0][0])
        part_i = merge_blocks(info, *part_i, flows_d, depth)
        part_d[0][0], part_i[0][0] = after(part_d[0][0], part_i[0][0])
    own_h, part_i[0][0] = after(own_h, part_i[0][0])
    whole = fold(info, [own_h, *others_h])[None]
    bit = spaces // 2
    whole = spread_step(whole, bit)
    own_d, others_d = turn_blocks(info, *part_d)
    part_i[0][0], own_d = after(part_i[0][0], own_d)
    own_i, others_i = turn_blocks(info, *part_i)
    whole, own_i = after(whole, own_i)
    while bit > 1:
        bit //= 2
        whole = spread_step(whole, bit)
    gathered = placed(info, whole)
    units = weight_in.shape[0] // devices
    head_rows = -(-out_width // devices)
    head_total = gathered[:, :head_rows].reshape(-1, width)[:out_width].T
    small = gathered[:SMALL, head_rows]
    in_mine = add_up(own_i, others_i)[:units]
    down_mine = add_up(own_d, others_d)[:units]
    return (in_mine, down_mine, head_total, small[9], small[:9])


def solution(mesh):
    return jax.shard_map(
        body,
        mesh=mesh,
        in_specs=(
            P("space", None, None),
            P("member", "space", None, None),
            P(),
            P(),
            P(),
            P(),
            P(),
            P("space", None, None),
        ),
        out_specs=(P(("member", "space"), None), P(("member", "space"), None), P(), P(), P()),
        check_vma=False,
    )
```

```python
import functools
import math

import jax
import jax.numpy as jnp
from jax import lax
from jax.experimental import pallas as pl
from jax.experimental.pallas import tpu as pltpu
from jax.sharding import PartitionSpec as P


F32 = jnp.float32
SMALL = 10
BF16 = jnp.bfloat16
LAST = (((1,), (1,)), ((), ()))
FIRST = (((0,), (0,)), ((), ()))
SMEM = pl.BlockSpec(memory_space=pltpu.SMEM)


def dot(left, right, dims=(((1,), (0,)), ((), ()))):
    return lax.dot_general(left, right, dims, preferred_element_type=F32)


def ring(count, step):
    return [(i, (i + step) % count) for i in range(count)]


def flip(count, bit):
    return [(i, i ^ bit) for i in range(count)]


def size_of(shape, kind):
    return math.prod(shape) * jnp.dtype(kind).itemsize


def call(kernel, ins, outs, scratch, micros, scalars=1, room=6):
    kept = sum(size_of(part.shape, part.dtype) for part in scratch)
    moved = sum(size_of(x.shape, x.dtype) for x in ins) + sum(size_of(*out) for out in outs)
    return pl.pallas_call(
        kernel,
        in_specs=[SMEM] * scalars
        + [pl.BlockSpec(memory_space=pltpu.VMEM)] * (len(ins) - scalars),
        out_specs=[pl.BlockSpec(memory_space=pltpu.VMEM)] * len(outs),
        out_shape=[jax.ShapeDtypeStruct(shape, kind) for shape, kind in outs],
        scratch_shapes=scratch,
        compiler_params=pltpu.CompilerParams(vmem_limit_bytes=kept + (room << 20)),
        cost_estimate=pl.CostEstimate(
            flops=int(micros * 1e9), bytes_accessed=moved, transcendentals=0
        ),
    )(*ins)


def tile_of(total):
    return next(t for t in range(640, 0, -128) if total % t == 0)


def mixed_row(mixed, edges, m, i):
    if i < 0:
        return edges[0][m, 0]
    if i >= mixed.shape[1]:
        return edges[1][m, 0]
    return mixed[m, i]


def forward_kernel(rows, members, members_all, edged, *refs):
    me_ref, mixed = refs[:2]
    edges = refs[2:4] if edged else ()
    conv_w, gain, w_in, w_down, w_head, target = refs[2 + len(edges) : 8 + len(edges)]
    rest = refs[8 + len(edges) :]
    normed, normal, inv, activ, slope, hidden, attract = rest[:7]
    sends = rest[7 : 7 + members]
    mix_s, pred = rest[7 + members :]
    mem_dev, _, lon, _ = mixed.shape
    span = len(rows) * lon
    tile = tile_of(w_in.shape[0])
    me = me_ref[0]

    def conv_step(m, carry):
        for at, i in enumerate(rows):
            start = pl.multiple_of(m * span + at * lon, lon)
            here = pl.ds(start, lon)
            sums = [None] * 3
            for a in range(3):
                row_b = mixed_row(mixed, edges, m, i + a - 1)
                if a == 1:
                    mix_s[here, :] = row_b
                row = row_b.astype(F32)
                for b in range(3):
                    k = 3 * a + b
                    term = conv_w[k : k + 1, :] * row
                    sums[b] = term if sums[b] is None else sums[b] + term
            conv = (
                sums[1] + pltpu.roll(sums[0], 1, axis=0) + pltpu.roll(sums[2], lon - 1, axis=0)
            )
            center = conv - jnp.mean(conv, axis=-1, keepdims=True)
            scale = lax.rsqrt(jnp.mean(center * center, axis=-1, keepdims=True) + 1e-05)
            unit = center * scale
            normal[here, :] = unit
            inv[here, :] = jnp.broadcast_to(scale, (lon, 128))
            normed[here, :] = (unit * gain[...]).astype(BF16)
        return carry

    lax.fori_loop(0, mem_dev, conv_step, 0)
    rate = math.sqrt(2.0 / math.pi)
    for t in range(w_in.shape[0] // tile):
        at = pl.ds(t * tile, tile)
        x = dot(normed[...], w_in[at, :], LAST)
        linear = rate * x
        bend = 1.0 + 0.044715 * (x * x)
        tanh = jnp.tanh(linear * bend)
        half = 0.5 + 0.5 * tanh
        activ[:, at] = (x * half).astype(BF16)
        slope[:, at] = (
            half * (1.0 + (1.0 - tanh) * (linear * (3.0 * bend - 2.0)))
        ).astype(BF16)
    hid = (mix_s[...].astype(F32) + dot(activ[...], w_down[...])).astype(BF16)
    hidden[...] = hid
    pred[...] = dot(hid, w_head[...], LAST)
    for m in range(mem_dev):
        for at, i in enumerate(rows):
            here = pl.ds(m * span + at * lon, lon)
            error = pred[here, :] - target[i].T
            dist = lax.rsqrt(jnp.sum(error * error, axis=-1, keepdims=True) + 1.0)
            attract[here, :] = error * dist * (1.0 / members_all)
    points = span // members
    for k in range(members):
        chunk = lax.rem(me + k, members)
        for m in range(mem_dev):
            at = pl.ds(pl.multiple_of(m * span + chunk * points, points), points)
            sends[k][m] = pred[at, :].astype(BF16)


def forward(me, mixed, edges, conv_w, gain, w_in, w_down, w_head, target, rows, members):
    mem_dev, _, lon, width = mixed.shape
    out_width = w_head.shape[0]
    units = w_in.shape[0]
    total = mem_dev * len(rows) * lon
    points = len(rows) * lon // members
    ins = [me, mixed, *edges, conv_w, gain, w_in, w_down, w_head, target]
    outs = [
        ((total, width), BF16),
        ((total, width), F32),
        ((total, 128), F32),
        ((total, units), BF16),
        ((total, units), BF16),
        ((total, width), BF16),
        ((total, out_width), F32),
    ] + [((mem_dev, points, out_width), BF16)] * members
    scratch = [
        pltpu.VMEM((total, width), BF16),
        pltpu.VMEM((total, out_width), F32),
    ]
    kernel = functools.partial(
        forward_kernel, rows, members, members * mem_dev, len(edges) > 0
    )
    out = call(kernel, ins, outs, scratch, 9)
    return out[:7], out[7:]


def pair_kernel(*refs):
    half = len(refs) // 2
    ins, outs = refs[:half], refs[half:]
    per, points = ins[0].shape[:2]
    step = 16 if points % 16 == 0 else points

    def run(t, carry):
        at = pl.ds(pl.multiple_of(t * step, step), step)
        values = [ref[m, at, :].astype(F32) for ref in ins for m in range(per)]
        pulls = [None] * len(values)
        for a in range(len(values)):
            for b in range(a + 1, len(values)):
                gap = values[a] - values[b]
                pull = gap * lax.rsqrt(jnp.sum(gap * gap, axis=-1, keepdims=True) + 1.0)
                pulls[a] = pull if pulls[a] is None else pulls[a] + pull
                pulls[b] = -pull if pulls[b] is None else pulls[b] - pull
        for index, pull in enumerate(pulls):
            outs[index // per][index % per, at, :] = pull.astype(BF16)
        return carry

    lax.fori_loop(0, points // step, run, 0)


def pair_pull(groups):
    return call(pair_kernel, groups, [(groups[0].shape, BF16)] * len(groups), [], 2, 0)


def slope_kernel(members, scale, share, *refs):
    me_ref, attract = refs[:2]
    pulls = refs[2 : 2 + members]
    w_head, w_down, slope, grad, ghid, gpre = refs[2 + members :]
    mem_dev, points, _ = pulls[0].shape
    span = attract.shape[0] // mem_dev
    tile = tile_of(w_down.shape[0])
    me = me_ref[0]
    for k in range(members):
        chunk = lax.rem(me + k, members)
        for m in range(mem_dev):
            at = pl.ds(pl.multiple_of(m * span + chunk * points, points), points)
            grad[at, :] = (scale * (attract[at, :] - pulls[k][m].astype(F32) * share)).astype(BF16)
    ghid[...] = dot(grad[...], w_head[...]).astype(BF16)

    for t in range(w_down.shape[0] // tile):
        at = pl.ds(t * tile, tile)
        back = dot(ghid[...], w_down[at, :], LAST)
        gpre[:, at] = (slope[:, at].astype(F32) * back).astype(BF16)


def slopes(me, attract, pulls, w_head, w_down, slope, scale, share):
    total, out_width = attract.shape
    outs = [
        ((total, out_width), BF16),
        ((total, w_head.shape[1]), BF16),
        (slope.shape, BF16),
    ]
    kernel = functools.partial(slope_kernel, len(pulls), scale, share)
    ins = [me, attract, *pulls, w_head, w_down, slope]
    return call(kernel, ins, outs, [], 3)


def norm_kernel(rows, edged, *refs):
    gpre, w_in, normal, inv, gain, mixed = refs[:6]
    edges = refs[6:8] if edged else ()
    small, acc = refs[6 + len(edges) :]
    mem_dev, _, lon, _ = mixed.shape
    span = len(rows) * lon
    acc[...] = dot(gpre[...], w_in[...])
    small[...] = jnp.zeros(small.shape, F32)

    def conv_step(m, carry):
        for at, i in enumerate(rows):
            here = pl.ds(pl.multiple_of(m * span + at * lon, lon), lon)
            back = acc[here, :]
            unit = normal[here, :]
            product = back * unit
            small[9:10, :] += jnp.sum(product, axis=0, keepdims=True)
            g = back * gain[...]
            mean = jnp.mean(g, axis=-1, keepdims=True)
            along = jnp.mean(product * gain[...], axis=-1, keepdims=True)
            out = (g - mean - unit * along) * inv[here, 0:1]
            turned = [pltpu.roll(out, lon - 1, axis=0), out, pltpu.roll(out, 1, axis=0)]
            for a in range(3):
                row = mixed_row(mixed, edges, m, i + a - 1).astype(F32)
                for b in range(3):
                    k = 3 * a + b
                    small[k : k + 1, :] += jnp.sum(row * turned[b], axis=0, keepdims=True)
        return carry

    lax.fori_loop(0, mem_dev, conv_step, 0)


def norms(gpre, w_in, normal, inv, gain, mixed, edges, rows):
    width = w_in.shape[1]
    ins = [gpre, w_in, normal, inv, gain, mixed, *edges]
    kernel = functools.partial(norm_kernel, rows, len(edges) > 0)
    scratch = [pltpu.VMEM(normal.shape, F32)]
    return call(kernel, ins, [((16, width), F32)], scratch, 5, 0)[0]


def emit(source, low, keep, send, j, per):
    rows = keep.shape[1]
    even = source[2 * j * per : 2 * j * per + rows, :]
    odd = source[(2 * j + 1) * per : (2 * j + 1) * per + rows, :]
    keep[j] = jnp.where(low, even, odd)
    send[j] = jnp.where(low, odd, even).astype(BF16)


def weight_kernel(units, info_ref, left_a, left_b, right_a, right_b, keep, send, acc):
    size = left_a.shape[1]
    tile = tile_of(size)
    low = info_ref[1] == 0
    acc[size:, :] = jnp.zeros((acc.shape[0] - size, acc.shape[1]), F32)
    done = 0
    for t in range(size // tile):
        at = pl.ds(t * tile, tile)
        acc[at, :] = dot(left_a[:, at], right_a[...], FIRST) + dot(
            left_b[:, at], right_b[...], FIRST
        )
        while done < keep.shape[0] and (
            t == size // tile - 1 or (2 * done + 1) * units + keep.shape[1] <= (t + 1) * tile
        ):
            emit(acc, low, keep, send, done, units)
            done += 1


def pad_to(value, unit):
    return -(-value // unit) * unit


def weights(info, left, right, devices):
    size = left[0].shape[1]
    width = right[0].shape[1]
    units = size // devices
    rows = pad_to(units, 16)
    scratch = [pltpu.VMEM((pad_to(size + rows - units, 8) + 8, width), F32)]
    outs = [((devices // 2, rows, width), F32), ((devices // 2, rows, width), BF16)]
    kernel = functools.partial(weight_kernel, units)
    return call(kernel, [info, *left, *right], outs, scratch, 6)


def head_kernel(head_rows, info_ref, *refs):
    grads, hids, smalls = refs[0:2], refs[2:4], refs[4:6]
    keep, send, plain, head = refs[6:]
    wide = grads[0].shape[1]
    plain[0:wide, :] = dot(grads[0][...], hids[0][...], FIRST) + dot(
        grads[1][...], hids[1][...], FIRST
    )
    small = smalls[0][...] + smalls[1][...]
    head[...] = jnp.zeros(head.shape, F32)
    slot = keep.shape[1]
    for block in range(head.shape[0] // slot):
        rows = min(head_rows, max(0, wide - block * head_rows))
        if rows:
            head[block * slot : block * slot + rows, :] = plain[
                block * head_rows : block * head_rows + rows, :
            ]
        if block < SMALL:
            at = block * slot + head_rows
            head[at : at + 1, :] = small[block : block + 1, :]
    low = info_ref[1] == 0
    for j in range(keep.shape[0]):
        emit(head, low, keep, send, j, slot)


def heads(info, grads, hids, smalls, devices):
    wide = grads[0].shape[1]
    width = hids[0].shape[1]
    head_rows = -(-wide // devices)
    slot = pad_to(head_rows + 1, 16)
    scratch = [pltpu.VMEM((wide, width), F32), pltpu.VMEM((devices * slot, width), F32)]
    outs = [((devices // 2, slot, width), F32), ((devices // 2, slot, width), BF16)]
    kernel = functools.partial(head_kernel, head_rows)
    return call(kernel, [info, *grads, *hids, *smalls], outs, scratch, 2)


def insert(index, place, bit):
    low = (1 << place) - 1
    return ((index >> place) << (place + 1)) | (bit << place) | (index & low)


def merge_kernel(plans, shared, info_ref, *refs):
    count = len(plans)
    given = 1 if shared else count
    keeps, gots = refs[:given], refs[given : 2 * given]
    outs = refs[2 * given :]
    if shared:
        keeps, gots = keeps * count, gots * count
    for flow, (first, rows, place, which) in enumerate(plans):
        bit = info_ref[1 + which]
        keep, got = keeps[flow], gots[flow]
        out_keep, out_send = outs[2 * flow : 2 * flow + 2]
        at = pl.ds(first, rows)

        def step(i, carry, keep=keep, got=got, out_keep=out_keep, out_send=out_send, at=at, place=place, bit=bit):
            mine = insert(i, place, bit)
            other = insert(i, place, 1 - bit)
            out_keep[i] = keep[mine, at, :] + got[mine, at, :].astype(F32)
            out_send[i] = (keep[other, at, :] + got[other, at, :].astype(F32)).astype(BF16)
            return carry

        lax.fori_loop(0, out_keep.shape[0], step, 0)


def merge(info, keeps, gots, plans):
    width = keeps[0].shape[2]
    outs = []
    for keep, (_, rows, _, _) in zip(keeps, plans):
        blocks = keep.shape[0] // 2
        outs += [((blocks, rows, width), F32), ((blocks, rows, width), BF16)]
    shared = keeps[0] is keeps[-1]
    kernel = functools.partial(merge_kernel, plans, shared)
    if shared:
        keeps, gots = keeps[:1], gots[:1]
    out = call(kernel, [info, *keeps, *gots], outs, [], 1)
    return out[0::2], out[1::2]


def turn_kernel(members, firsts, info_ref, *refs):
    count = len(firsts)
    keeps, gots = refs[:count], refs[count : 2 * count]
    outs = refs[2 * count :]
    for k in range(members):
        block = lax.rem(info_ref[0] + k, members)
        for flow, first in enumerate(firsts):
            value = keeps[flow][block] + gots[flow][block].astype(F32)
            outs[k][first : first + value.shape[0], :] = value.astype(outs[k].dtype)


def turn(info, keeps, gots, members):
    width = keeps[0].shape[2]
    firsts, rows = [], 0
    for keep in keeps:
        firsts.append(rows)
        rows += keep.shape[1]
    outs = [((rows, width), F32)] + [((rows, width), BF16)] * (members - 1)
    kernel = functools.partial(turn_kernel, members, tuple(firsts))
    return call(kernel, [info, *keeps, *gots], outs, [], 1)


def start_blocks(send):
    return lax.ppermute(send, "space", flip(lax.axis_size("space"), 1))


def flows_of(rows):
    levels = list(range(1, lax.axis_size("space").bit_length() - 1))
    cut = pad_to(rows, 32) // 2
    flows = [(0, cut, levels)]
    if rows > cut:
        flows.append((cut, rows - cut, levels[::-1]))
    return flows


def merge_blocks(info, keeps, gots, flows, depth):
    spaces = lax.axis_size("space")
    plans = []
    for first, size, order in flows:
        place = sum(1 for other in order[depth:] if other < order[depth])
        plans.append((first if depth == 0 else 0, size, place, order[depth]))
    keeps, sends = merge(info, keeps, gots, tuple(plans))
    gots = [
        lax.ppermute(part, "space", flip(spaces, 1 << order[depth]))
        for part, (_, _, order) in zip(sends, flows)
    ]
    return list(keeps), list(gots)


def turn_blocks(info, keeps, gots):
    members = lax.axis_size("member")
    parts = turn(info, keeps, gots, members)
    return parts[0], [
        lax.ppermute(parts[k], "member", ring(members, k)) for k in range(1, members)
    ]


def add_up(own, others):
    for other in others:
        own = own + other.astype(F32)
    return own


def round_kernel(info_ref, keep, got, own):
    own[...] = (keep[...] + got[...].astype(F32)).astype(BF16)


def fold_kernel(info_ref, *refs):
    pieces, out, hold = refs[:-2], refs[-2], refs[-1]
    members = len(pieces)
    for k in range(members):
        hold[k] = pieces[k][...].astype(F32)
    total = hold[info_ref[0]]
    for m in range(1, members):
        total = total + hold[lax.rem(info_ref[0] + members - m, members)]
    out[...] = total.astype(BF16)


def turned(index, count):
    bits = count.bit_length() - 1
    return sum(((index >> b) & 1) << (bits - 1 - b) for b in range(bits))


def place_kernel(info_ref, rel, head, conv, gain, hold):
    spaces, members = rel.shape[:2]
    place = 0
    for bit in range(spaces.bit_length() - 1):
        place = place + info_ref[1 + bit] * (1 << bit)
    for r in range(spaces):
        for m in range(members):
            hold[m * spaces + (place ^ turned(r, spaces))] = rel[r, m].astype(F32)
    wide = head.shape[0]
    rows = -(-wide // (members * spaces))
    for block in range(members * spaces):
        size = min(rows, wide - block * rows)
        if size > 0:
            head[block * rows : block * rows + size, :] = hold[block, 0:size, :]
        if block < SMALL - 1:
            conv[block : block + 1, :] = hold[block, rows : rows + 1, :]
        elif block == SMALL - 1:
            gain[...] = hold[block, rows : rows + 1, :]


def fold_members(info, keep, got):
    members = lax.axis_size("member")
    own = call(round_kernel, [info, keep, got], [(keep.shape, BF16)], [], 1)[0]
    return own, [lax.ppermute(own, "member", ring(members, k)) for k in range(1, members)]


def fold(info, pieces):
    scratch = [pltpu.VMEM((len(pieces),) + pieces[0].shape, F32)]
    return call(fold_kernel, [info, *pieces], [(pieces[0].shape, BF16)], scratch, 1)[0]


def spread_step(whole, bit):
    other = lax.ppermute(whole, "space", flip(lax.axis_size("space"), bit))
    return jnp.concatenate([whole, other], axis=0)


def placed(info, whole, wide):
    spaces, members = whole.shape[:2]
    width = whole.shape[3]
    outs = [((wide, width), F32), ((SMALL - 1, width), F32), ((1, width), F32)]
    scratch = [pltpu.VMEM((members * spaces,) + whole.shape[2:], F32)]
    return call(place_kernel, [info, whole], outs, scratch, 1)


def after(value, other):
    return lax.optimization_barrier((value, other))


def mix_kernel(info_ref, latent, noise, mixed, first, last):
    mem_dev, lat = noise.shape[:2]
    for i in range(lat):
        for m in range(mem_dev):
            value = (latent[i].astype(F32) + noise[m, i].astype(F32)).astype(BF16)
            mixed[m, i] = value
            if i == 0:
                first[m, 0] = value
            if i == lat - 1:
                last[m, 0] = value


def mix_rows(info, latent, noise):
    mem_dev, _, lon, width = noise.shape
    edge = ((mem_dev, 1, lon, width), BF16)
    outs = [(noise.shape, BF16), edge, edge]
    return call(mix_kernel, [info, latent, noise], outs, [], 20)


def body(
    latent_state,
    member_noise,
    conv_weight,
    norm_gain,
    weight_in,
    weight_down,
    weight_head,
    target_field,
):
    mem_dev, lat_dev, lon_len, width = member_noise.shape
    out_width = weight_head.shape[1]
    members = lax.axis_size("member")
    spaces = lax.axis_size("space")
    devices = members * spaces
    members_all = mem_dev * members
    points_all = lat_dev * spaces * lon_len
    scale = math.sqrt(members_all * out_width / points_all)
    share = 1.0 / (members_all * (members_all - 1))
    place = lax.axis_index("space")
    info = jnp.stack(
        [lax.axis_index("member")] + [(place >> b) & 1 for b in range(spaces.bit_length() - 1)]
    ).astype(jnp.int32)
    gain = norm_gain.reshape(1, width)
    head_t = weight_head.T
    target_t = target_field.transpose(0, 2, 1)

    mixed, first, last = mix_rows(info, latent_state, member_noise)
    above = lax.ppermute(last, "space", [(i, i + 1) for i in range(spaces - 1)])
    below = lax.ppermute(first, "space", [(i + 1, i) for i in range(spaces - 1)])
    halves = [(tuple(range(1, lat_dev - 1)), ()), ((0, lat_dev - 1), (above, below))]

    saved, pulled = [], []
    for rows, edges in halves:
        kept, sends = forward(
            info, mixed, edges, conv_weight, gain,
            weight_in, weight_down, head_t, target_t, rows, members,
        )
        saved.append(kept)
        pulled.append(
            [sends[0]]
            + [lax.ppermute(sends[k], "member", ring(members, k)) for k in range(1, members)]
        )
    pulled[0][-1], pulled[1][0] = lax.optimization_barrier((pulled[0][-1], pulled[1][0]))
    backs = []
    for half in range(2):
        pulls = pair_pull(pulled[half])
        backs.append(
            [pulls[0]]
            + [
                lax.ppermute(pulls[k], "member", ring(members, members - k))
                for k in range(1, members)
            ]
        )
    backs[0][0], backs[1][0] = lax.optimization_barrier((backs[0][0], backs[1][0]))
    grads, smalls = [], []
    for half, (rows, edges) in enumerate(halves):
        _, normal, inv, _, slope, _, attract = saved[half]
        if half:
            attract, smalls[0] = lax.optimization_barrier((attract, smalls[0]))
        grads.append(
            slopes(info, attract, backs[half], head_t, weight_down, slope, scale, share)
        )
        if half == 0:
            smalls.append(
                norms(grads[0][2], weight_in, normal, inv, gain, mixed, edges, rows)
            )

    hids = [saved[h][5] for h in range(2)]
    depths = spaces.bit_length() - 2
    rows, edges = halves[1]
    normal, inv = saved[1][1:3]
    smalls.append(norms(grads[1][2], weight_in, normal, inv, gain, mixed, edges, rows))
    keep_h, send_h = heads(info, [grads[h][0] for h in range(2)], hids, smalls, devices)
    got_h = start_blocks(send_h)
    keep_d, send_d = weights(
        info, [saved[h][3] for h in range(2)], [grads[h][1] for h in range(2)], devices
    )
    got_d = start_blocks(send_d)
    flows_h, flows_d = flows_of(keep_h.shape[1]), flows_of(keep_d.shape[1])
    keep_h, keep_d = after(keep_h, keep_d)
    part_h = merge_blocks(info, [keep_h], [got_h], flows_h, 0)
    gpre = [grads[h][2] for h in range(2)]
    gpre[1], part_h[0][0] = after(gpre[1], part_h[0][0])
    keep_i, send_i = weights(info, gpre, [saved[h][0] for h in range(2)], devices)
    got_i = start_blocks(send_i)
    part_h[0][0], keep_i = after(part_h[0][0], keep_i)
    for depth in range(1, depths):
        part_h = merge_blocks(info, *part_h, flows_h, depth)
    keep_d, part_h[0][0] = after(keep_d, part_h[0][0])
    part_d = [keep_d] * len(flows_d), [got_d] * len(flows_d)
    part_d = merge_blocks(info, *part_d, flows_d, 0)
    keep_i, part_d[0][0] = after(keep_i, part_d[0][0])
    part_i = [keep_i] * len(flows_d), [got_i] * len(flows_d)
    part_i = merge_blocks(info, *part_i, flows_d, 0)
    part_h[0][0], part_i[0][0] = after(part_h[0][0], part_i[0][0])
    own_h, others_h = fold_members(info, part_h[0][0], part_h[1][0])
    part_d[0][0], own_h = after(part_d[0][0], own_h)
    for depth in range(1, depths):
        part_d = merge_blocks(info, *part_d, flows_d, depth)
    own_h, part_d[0][0] = after(own_h, part_d[0][0])
    whole = fold(info, [own_h, *others_h])[None]
    bit = spaces // 2
    part_i[0][0], whole = after(part_i[0][0], whole)
    whole = spread_step(whole, bit)
    for depth in range(1, depths):
        part_i = merge_blocks(info, *part_i, flows_d, depth)
    part_d[0][0], part_i[0][0] = after(part_d[0][0], part_i[0][0])
    own_d, others_d = turn_blocks(info, *part_d)
    part_i[0][0], own_d = after(part_i[0][0], own_d)
    whole, own_d = after(whole, own_d)
    while bit > 2:
        bit //= 2
        whole = spread_step(whole, bit)
    own_i, others_i = turn_blocks(info, *part_i)
    whole, own_i = after(whole, own_i)
    whole = spread_step(whole, 1)
    units = weight_in.shape[0] // devices
    head_total, conv_total, gain_total = placed(info, whole, out_width)
    in_mine = add_up(own_i, others_i)[:units]
    down_mine = add_up(own_d, others_d)[:units]
    return (in_mine, down_mine, head_total.T, gain_total.reshape(width), conv_total)


def solution(mesh):
    return jax.shard_map(
        body,
        mesh=mesh,
        in_specs=(
            P("space", None, None),
            P("member", "space", None, None),
            P(),
            P(),
            P(),
            P(),
            P(),
            P("space", None, None),
        ),
        out_specs=(P(("member", "space"), None), P(("member", "space"), None), P(), P(), P()),
        check_vma=False,
    )
```

```python
import functools
import math

import jax
import jax.numpy as jnp
from jax import lax
from jax.experimental import pallas as pl
from jax.experimental.pallas import tpu as pltpu
from jax.sharding import PartitionSpec as P


F32 = jnp.float32
SMALL = 10
BF16 = jnp.bfloat16
LAST = (((1,), (1,)), ((), ()))
FIRST = (((0,), (0,)), ((), ()))
SMEM = pl.BlockSpec(memory_space=pltpu.SMEM)


def dot(left, right, dims=(((1,), (0,)), ((), ()))):
    return lax.dot_general(left, right, dims, preferred_element_type=F32)


def ring(count, step):
    return [(i, (i + step) % count) for i in range(count)]


def flip(count, bit):
    return [(i, i ^ bit) for i in range(count)]


def size_of(shape, kind):
    return math.prod(shape) * jnp.dtype(kind).itemsize


def call(kernel, ins, outs, scratch, micros, scalars=1, room=6):
    kept = sum(size_of(part.shape, part.dtype) for part in scratch)
    moved = sum(size_of(x.shape, x.dtype) for x in ins) + sum(size_of(*out) for out in outs)
    return pl.pallas_call(
        kernel,
        in_specs=[SMEM] * scalars
        + [pl.BlockSpec(memory_space=pltpu.VMEM)] * (len(ins) - scalars),
        out_specs=[pl.BlockSpec(memory_space=pltpu.VMEM)] * len(outs),
        out_shape=[jax.ShapeDtypeStruct(shape, kind) for shape, kind in outs],
        scratch_shapes=scratch,
        compiler_params=pltpu.CompilerParams(vmem_limit_bytes=kept + (room << 20)),
        cost_estimate=pl.CostEstimate(
            flops=int(micros * 1e9), bytes_accessed=moved, transcendentals=0
        ),
    )(*ins)


def tile_of(total):
    return next(t for t in range(640, 0, -128) if total % t == 0)


def mixed_row(mixed, edges, m, i):
    if i < 0:
        return edges[0][m, 0]
    if i >= mixed.shape[1]:
        return edges[1][m, 0]
    return mixed[m, i]


def first_part(rows, mixed, edges, conv_w, gain, w_in, normed, normal, inv, activ, slope):
    mem_dev, _, lon, _ = mixed.shape
    span = len(rows) * lon
    tile = tile_of(w_in.shape[0])

    def conv_step(m, carry):
        for at, i in enumerate(rows):
            here = pl.ds(pl.multiple_of(m * span + at * lon, lon), lon)
            sums = [None] * 3
            for a in range(3):
                row = mixed_row(mixed, edges, m, i + a - 1).astype(F32)
                for b in range(3):
                    k = 3 * a + b
                    term = conv_w[k : k + 1, :] * row
                    sums[b] = term if sums[b] is None else sums[b] + term
            conv = (
                sums[1] + pltpu.roll(sums[0], 1, axis=0) + pltpu.roll(sums[2], lon - 1, axis=0)
            )
            center = conv - jnp.mean(conv, axis=-1, keepdims=True)
            scale = lax.rsqrt(jnp.mean(center * center, axis=-1, keepdims=True) + 1e-05)
            unit = center * scale
            normal[here, :] = unit
            inv[here, :] = jnp.broadcast_to(scale, (lon, 128))
            normed[here, :] = (unit * gain[...]).astype(BF16)
        return carry

    lax.fori_loop(0, mem_dev, conv_step, 0)
    rate = math.sqrt(2.0 / math.pi)
    for t in range(w_in.shape[0] // tile):
        at = pl.ds(t * tile, tile)
        x = dot(normed[...], w_in[at, :], LAST)
        linear = rate * x
        bend = 1.0 + 0.044715 * (x * x)
        tanh = jnp.tanh(linear * bend)
        half = 0.5 + 0.5 * tanh
        activ[:, at] = (x * half).astype(BF16)
        slope[:, at] = (
            half * (1.0 + (1.0 - tanh) * (linear * (3.0 * bend - 2.0)))
        ).astype(BF16)


def last_part(
    rows, members_all, info_ref, mixed, activ, w_down, w_head, target, hidden, attract, sends, pred
):
    mem_dev, _, lon, _ = mixed.shape
    members = len(sends)
    span = len(rows) * lon
    down = dot(activ[...], w_down[...])
    for m in range(mem_dev):
        for at, i in enumerate(rows):
            first = m * span + at * lon
            hidden[first : first + lon, :] = (
                mixed[m, i].astype(F32) + down[first : first + lon, :]
            ).astype(BF16)
    pred[...] = dot(hidden[...], w_head[...], LAST)
    for m in range(mem_dev):
        for at, i in enumerate(rows):
            here = pl.ds(m * span + at * lon, lon)
            error = pred[here, :] - target[i].T
            dist = lax.rsqrt(jnp.sum(error * error, axis=-1, keepdims=True) + 1.0)
            attract[here, :] = error * dist * (1.0 / members_all)
    points = span // members
    for k in range(members):
        chunk = lax.rem(info_ref[0] + k, members)
        for m in range(mem_dev):
            at = pl.ds(pl.multiple_of(m * span + chunk * points, points), points)
            sends[k][m] = pred[at, :].astype(BF16)


def forward_kernel(rows, members_all, *refs):
    info_ref, mixed, conv_w, gain, w_in, w_down, w_head, target = refs[:8]
    outs, (pred,) = refs[8:-1], refs[-1:]
    normed, normal, inv, activ, slope, hidden, attract = outs[:7]
    first_part(rows, mixed, (), conv_w, gain, w_in, normed, normal, inv, activ, slope)
    last_part(
        rows, members_all, info_ref, mixed, activ, w_down, w_head, target, hidden, attract,
        outs[7:], pred,
    )


def begin_kernel(rows, info_ref, mixed, above, below, *refs):
    first_part(rows, mixed, (above, below), *refs)


def finish_kernel(rows, members_all, *refs):
    info_ref, mixed, activ, w_down, w_head, target, hidden, attract = refs[:8]
    last_part(
        rows, members_all, info_ref, mixed, activ, w_down, w_head, target, hidden, attract,
        refs[8:-1], refs[-1],
    )


def forward_shapes(mixed, w_in, w_head, rows, members):
    mem_dev, _, lon, width = mixed.shape
    out_width, units = w_head.shape[0], w_in.shape[0]
    total = mem_dev * len(rows) * lon
    points = len(rows) * lon // members
    early = [
        ((total, width), BF16),
        ((total, width), F32),
        ((total, 128), F32),
        ((total, units), BF16),
        ((total, units), BF16),
    ]
    late = [((total, width), BF16), ((total, out_width), F32)]
    late += [((mem_dev, points, out_width), BF16)] * members
    return early, late, [pltpu.VMEM((total, out_width), F32)]


def forward(info, mixed, conv_w, gain, w_in, w_down, w_head, target, rows, members):
    early, late, scratch = forward_shapes(mixed, w_in, w_head, rows, members)
    kernel = functools.partial(forward_kernel, rows, members * mixed.shape[0])
    ins = [info, mixed, conv_w, gain, w_in, w_down, w_head, target]
    out = call(kernel, ins, early + late, scratch, 9)
    return out[:7], out[7:]


def begin(info, mixed, edges, conv_w, gain, w_in, w_head, rows, members):
    early = forward_shapes(mixed, w_in, w_head, rows, members)[0]
    kernel = functools.partial(begin_kernel, rows)
    return call(kernel, [info, mixed, *edges, conv_w, gain, w_in], early, [], 6)


def finish(info, mixed, activ, w_in, w_down, w_head, target, rows, members):
    _, late, scratch = forward_shapes(mixed, w_in, w_head, rows, members)
    kernel = functools.partial(finish_kernel, rows, members * mixed.shape[0])
    ins = [info, mixed, activ, w_down, w_head, target]
    out = call(kernel, ins, late, scratch, 2)
    return out[:2], out[2:]


def pair_kernel(*refs):
    half = len(refs) // 2
    ins, outs = refs[:half], refs[half:]
    per, points = ins[0].shape[:2]
    step = 16 if points % 16 == 0 else points

    def run(t, carry):
        at = pl.ds(pl.multiple_of(t * step, step), step)
        values = [ref[m, at, :].astype(F32) for ref in ins for m in range(per)]
        pulls = [None] * len(values)
        for a in range(len(values)):
            for b in range(a + 1, len(values)):
                gap = values[a] - values[b]
                pull = gap * lax.rsqrt(jnp.sum(gap * gap, axis=-1, keepdims=True) + 1.0)
                pulls[a] = pull if pulls[a] is None else pulls[a] + pull
                pulls[b] = -pull if pulls[b] is None else pulls[b] - pull
        for index, pull in enumerate(pulls):
            outs[index // per][index % per, at, :] = pull.astype(BF16)
        return carry

    lax.fori_loop(0, points // step, run, 0)


def pair_pull(groups):
    return call(pair_kernel, groups, [(groups[0].shape, BF16)] * len(groups), [], 2, 0)


def slope_kernel(members, scale, share, *refs):
    me_ref, attract = refs[:2]
    pulls = refs[2 : 2 + members]
    w_head, w_down, slope, grad, ghid, gpre = refs[2 + members :]
    mem_dev, points, _ = pulls[0].shape
    span = attract.shape[0] // mem_dev
    tile = tile_of(w_down.shape[0])
    me = me_ref[0]
    for k in range(members):
        chunk = lax.rem(me + k, members)
        for m in range(mem_dev):
            at = pl.ds(pl.multiple_of(m * span + chunk * points, points), points)
            grad[at, :] = (scale * (attract[at, :] - pulls[k][m].astype(F32) * share)).astype(BF16)
    ghid[...] = dot(grad[...], w_head[...]).astype(BF16)

    for t in range(w_down.shape[0] // tile):
        at = pl.ds(t * tile, tile)
        back = dot(ghid[...], w_down[at, :], LAST)
        gpre[:, at] = (slope[:, at].astype(F32) * back).astype(BF16)


def slopes(me, attract, pulls, w_head, w_down, slope, scale, share):
    total, out_width = attract.shape
    outs = [
        ((total, out_width), BF16),
        ((total, w_head.shape[1]), BF16),
        (slope.shape, BF16),
    ]
    kernel = functools.partial(slope_kernel, len(pulls), scale, share)
    ins = [me, attract, *pulls, w_head, w_down, slope]
    return call(kernel, ins, outs, [], 3)


def norm_kernel(rows, edged, *refs):
    gpre, w_in, normal, inv, gain, mixed = refs[:6]
    edges = refs[6:8] if edged else ()
    small, acc = refs[6 + len(edges) :]
    mem_dev, _, lon, _ = mixed.shape
    span = len(rows) * lon
    acc[...] = dot(gpre[...], w_in[...])
    small[...] = jnp.zeros(small.shape, F32)

    def conv_step(m, carry):
        for at, i in enumerate(rows):
            here = pl.ds(pl.multiple_of(m * span + at * lon, lon), lon)
            back = acc[here, :]
            unit = normal[here, :]
            product = back * unit
            small[9:10, :] += jnp.sum(product, axis=0, keepdims=True)
            g = back * gain[...]
            mean = jnp.mean(g, axis=-1, keepdims=True)
            along = jnp.mean(product * gain[...], axis=-1, keepdims=True)
            out = (g - mean - unit * along) * inv[here, 0:1]
            turned = [pltpu.roll(out, lon - 1, axis=0), out, pltpu.roll(out, 1, axis=0)]
            for a in range(3):
                row = mixed_row(mixed, edges, m, i + a - 1).astype(F32)
                for b in range(3):
                    k = 3 * a + b
                    small[k : k + 1, :] += jnp.sum(row * turned[b], axis=0, keepdims=True)
        return carry

    lax.fori_loop(0, mem_dev, conv_step, 0)


def norms(gpre, w_in, normal, inv, gain, mixed, edges, rows):
    width = w_in.shape[1]
    ins = [gpre, w_in, normal, inv, gain, mixed, *edges]
    kernel = functools.partial(norm_kernel, rows, len(edges) > 0)
    scratch = [pltpu.VMEM(normal.shape, F32)]
    return call(kernel, ins, [((16, width), F32)], scratch, 5, 0)[0]


def emit(source, low, keep, send, j, per):
    rows = keep.shape[1]
    even = source[2 * j * per : 2 * j * per + rows, :]
    odd = source[(2 * j + 1) * per : (2 * j + 1) * per + rows, :]
    keep[j] = jnp.where(low, even, odd)
    send[j] = jnp.where(low, odd, even).astype(BF16)


def weight_kernel(units, info_ref, left_a, left_b, right_a, right_b, keep, send, acc):
    size = left_a.shape[1]
    tile = tile_of(size)
    low = info_ref[1] == 0
    acc[size:, :] = jnp.zeros((acc.shape[0] - size, acc.shape[1]), F32)
    done = 0
    for t in range(size // tile):
        at = pl.ds(t * tile, tile)
        acc[at, :] = dot(left_a[:, at], right_a[...], FIRST) + dot(
            left_b[:, at], right_b[...], FIRST
        )
        while done < keep.shape[0] and (
            t == size // tile - 1 or (2 * done + 1) * units + keep.shape[1] <= (t + 1) * tile
        ):
            emit(acc, low, keep, send, done, units)
            done += 1


def pad_to(value, unit):
    return -(-value // unit) * unit


def weights(info, left, right, devices):
    size = left[0].shape[1]
    width = right[0].shape[1]
    units = size // devices
    rows = pad_to(units, 16)
    scratch = [pltpu.VMEM((pad_to(size + rows - units, 8) + 8, width), F32)]
    outs = [((devices // 2, rows, width), F32), ((devices // 2, rows, width), BF16)]
    kernel = functools.partial(weight_kernel, units)
    return call(kernel, [info, *left, *right], outs, scratch, 6)


def head_kernel(head_rows, info_ref, *refs):
    grads, hids, smalls = refs[0:2], refs[2:4], refs[4:6]
    keep, send, plain, head = refs[6:]
    wide = grads[0].shape[1]
    plain[0:wide, :] = dot(grads[0][...], hids[0][...], FIRST) + dot(
        grads[1][...], hids[1][...], FIRST
    )
    small = smalls[0][...] + smalls[1][...]
    head[...] = jnp.zeros(head.shape, F32)
    slot = keep.shape[1]
    for block in range(head.shape[0] // slot):
        rows = min(head_rows, max(0, wide - block * head_rows))
        if rows:
            head[block * slot : block * slot + rows, :] = plain[
                block * head_rows : block * head_rows + rows, :
            ]
        if block < SMALL:
            at = block * slot + head_rows
            head[at : at + 1, :] = small[block : block + 1, :]
    low = info_ref[1] == 0
    for j in range(keep.shape[0]):
        emit(head, low, keep, send, j, slot)


def heads(info, grads, hids, smalls, devices):
    wide = grads[0].shape[1]
    width = hids[0].shape[1]
    head_rows = -(-wide // devices)
    slot = pad_to(head_rows + 1, 16)
    scratch = [pltpu.VMEM((wide, width), F32), pltpu.VMEM((devices * slot, width), F32)]
    outs = [((devices // 2, slot, width), F32), ((devices // 2, slot, width), BF16)]
    kernel = functools.partial(head_kernel, head_rows)
    return call(kernel, [info, *grads, *hids, *smalls], outs, scratch, 2)


def insert(index, place, bit):
    low = (1 << place) - 1
    return ((index >> place) << (place + 1)) | (bit << place) | (index & low)


def merge_kernel(plans, shared, info_ref, *refs):
    count = len(plans)
    given = 1 if shared else count
    keeps, gots = refs[:given], refs[given : 2 * given]
    outs = refs[2 * given :]
    if shared:
        keeps, gots = keeps * count, gots * count
    for flow, (first, rows, place, which) in enumerate(plans):
        bit = info_ref[1 + which]
        keep, got = keeps[flow], gots[flow]
        out_keep, out_send = outs[2 * flow : 2 * flow + 2]
        at = pl.ds(first, rows)

        def step(i, carry, keep=keep, got=got, out_keep=out_keep, out_send=out_send, at=at, place=place, bit=bit):
            mine = insert(i, place, bit)
            other = insert(i, place, 1 - bit)
            out_keep[i] = keep[mine, at, :] + got[mine, at, :].astype(F32)
            out_send[i] = (keep[other, at, :] + got[other, at, :].astype(F32)).astype(BF16)
            return carry

        lax.fori_loop(0, out_keep.shape[0], step, 0)


def merge(info, keeps, gots, plans):
    width = keeps[0].shape[2]
    outs = []
    for keep, (_, rows, _, _) in zip(keeps, plans):
        blocks = keep.shape[0] // 2
        outs += [((blocks, rows, width), F32), ((blocks, rows, width), BF16)]
    shared = keeps[0] is keeps[-1]
    kernel = functools.partial(merge_kernel, plans, shared)
    if shared:
        keeps, gots = keeps[:1], gots[:1]
    out = call(kernel, [info, *keeps, *gots], outs, [], 1)
    return out[0::2], out[1::2]


def turn_kernel(members, firsts, info_ref, *refs):
    count = len(firsts)
    keeps, gots = refs[:count], refs[count : 2 * count]
    outs = refs[2 * count :]
    for k in range(members):
        block = lax.rem(info_ref[0] + k, members)
        for flow, first in enumerate(firsts):
            value = keeps[flow][block] + gots[flow][block].astype(F32)
            outs[k][first : first + value.shape[0], :] = value.astype(outs[k].dtype)


def turn(info, keeps, gots, members):
    width = keeps[0].shape[2]
    firsts, rows = [], 0
    for keep in keeps:
        firsts.append(rows)
        rows += keep.shape[1]
    outs = [((rows, width), F32)] + [((rows, width), BF16)] * (members - 1)
    kernel = functools.partial(turn_kernel, members, tuple(firsts))
    return call(kernel, [info, *keeps, *gots], outs, [], 1)


def start_blocks(send):
    return lax.ppermute(send, "space", flip(lax.axis_size("space"), 1))


def flows_of(rows):
    levels = list(range(1, lax.axis_size("space").bit_length() - 1))
    cut = pad_to(rows, 32) // 2
    flows = [(0, cut, levels)]
    if rows > cut:
        flows.append((cut, rows - cut, levels[::-1]))
    return flows


def merge_blocks(info, keeps, gots, flows, depth):
    spaces = lax.axis_size("space")
    plans = []
    for first, size, order in flows:
        place = sum(1 for other in order[depth:] if other < order[depth])
        plans.append((first if depth == 0 else 0, size, place, order[depth]))
    keeps, sends = merge(info, keeps, gots, tuple(plans))
    gots = [
        lax.ppermute(part, "space", flip(spaces, 1 << order[depth]))
        for part, (_, _, order) in zip(sends, flows)
    ]
    return list(keeps), list(gots)


def turn_blocks(info, keeps, gots):
    members = lax.axis_size("member")
    parts = turn(info, keeps, gots, members)
    return parts[0], [
        lax.ppermute(parts[k], "member", ring(members, k)) for k in range(1, members)
    ]


def add_up(own, others):
    for other in others:
        own = own + other.astype(F32)
    return own


def round_kernel(info_ref, keep, got, own):
    own[...] = (keep[...] + got[...].astype(F32)).astype(BF16)


def fold_kernel(info_ref, *refs):
    pieces, out, hold = refs[:-2], refs[-2], refs[-1]
    members = len(pieces)
    for k in range(members):
        hold[k] = pieces[k][...].astype(F32)
    total = hold[info_ref[0]]
    for m in range(1, members):
        total = total + hold[lax.rem(info_ref[0] + members - m, members)]
    out[...] = total.astype(BF16)


def turned(index, count):
    bits = count.bit_length() - 1
    return sum(((index >> b) & 1) << (bits - 1 - b) for b in range(bits))


def place_kernel(info_ref, rel, head, conv, gain, hold):
    spaces, members = rel.shape[:2]
    place = 0
    for bit in range(spaces.bit_length() - 1):
        place = place + info_ref[1 + bit] * (1 << bit)
    for r in range(spaces):
        for m in range(members):
            hold[m * spaces + (place ^ turned(r, spaces))] = rel[r, m].astype(F32)
    wide = head.shape[0]
    rows = -(-wide // (members * spaces))
    for block in range(members * spaces):
        size = min(rows, wide - block * rows)
        if size > 0:
            head[block * rows : block * rows + size, :] = hold[block, 0:size, :]
        if block < SMALL - 1:
            conv[block : block + 1, :] = hold[block, rows : rows + 1, :]
        elif block == SMALL - 1:
            gain[...] = hold[block, rows : rows + 1, :]


def fold_members(info, keep, got):
    members = lax.axis_size("member")
    own = call(round_kernel, [info, keep, got], [(keep.shape, BF16)], [], 1)[0]
    return own, [lax.ppermute(own, "member", ring(members, k)) for k in range(1, members)]


def fold(info, pieces):
    scratch = [pltpu.VMEM((len(pieces),) + pieces[0].shape, F32)]
    return call(fold_kernel, [info, *pieces], [(pieces[0].shape, BF16)], scratch, 1)[0]


def spread_step(whole, bit):
    other = lax.ppermute(whole, "space", flip(lax.axis_size("space"), bit))
    return jnp.concatenate([whole, other], axis=0)


def placed(info, whole, wide):
    spaces, members = whole.shape[:2]
    width = whole.shape[3]
    outs = [((wide, width), F32), ((SMALL - 1, width), F32), ((1, width), F32)]
    scratch = [pltpu.VMEM((members * spaces,) + whole.shape[2:], F32)]
    return call(place_kernel, [info, whole], outs, scratch, 1)


def after(value, other):
    return lax.optimization_barrier((value, other))


def mix_kernel(info_ref, latent, noise, mixed, first, last):
    mem_dev, lat = noise.shape[:2]
    for i in range(lat):
        for m in range(mem_dev):
            value = (latent[i].astype(F32) + noise[m, i].astype(F32)).astype(BF16)
            mixed[m, i] = value
            if i == 0:
                first[m, 0] = value
            if i == lat - 1:
                last[m, 0] = value


def mix_rows(info, latent, noise):
    mem_dev, _, lon, width = noise.shape
    edge = ((mem_dev, 1, lon, width), BF16)
    outs = [(noise.shape, BF16), edge, edge]
    return call(mix_kernel, [info, latent, noise], outs, [], 20)


def body(
    latent_state,
    member_noise,
    conv_weight,
    norm_gain,
    weight_in,
    weight_down,
    weight_head,
    target_field,
):
    mem_dev, lat_dev, lon_len, width = member_noise.shape
    out_width = weight_head.shape[1]
    members = lax.axis_size("member")
    spaces = lax.axis_size("space")
    devices = members * spaces
    members_all = mem_dev * members
    points_all = lat_dev * spaces * lon_len
    scale = math.sqrt(members_all * out_width / points_all)
    share = 1.0 / (members_all * (members_all - 1))
    place = lax.axis_index("space")
    info = jnp.stack(
        [lax.axis_index("member")] + [(place >> b) & 1 for b in range(spaces.bit_length() - 1)]
    ).astype(jnp.int32)
    gain = norm_gain.reshape(1, width)
    head_t = weight_head.T
    target_t = target_field.transpose(0, 2, 1)

    mixed, first, last = mix_rows(info, latent_state, member_noise)
    above = lax.ppermute(last, "space", [(i, i + 1) for i in range(spaces - 1)])
    below = lax.ppermute(first, "space", [(i + 1, i) for i in range(spaces - 1)])
    halves = [(tuple(range(1, lat_dev - 1)), ()), ((0, lat_dev - 1), (above, below))]

    def exchange(sends):
        return [sends[0]] + [
            lax.ppermute(sends[k], "member", ring(members, k)) for k in range(1, members)
        ]

    def give_back(pulls):
        return [pulls[0]] + [
            lax.ppermute(pulls[k], "member", ring(members, members - k))
            for k in range(1, members)
        ]

    rows_a, rows_b = halves[0][0], halves[1][0]
    kept_a, sends = forward(
        info, mixed, conv_weight, gain, weight_in, weight_down, head_t, target_t, rows_a, members
    )
    pulled_a = exchange(sends)
    kept_b = begin(
        info, mixed, (above, below), conv_weight, gain, weight_in, head_t, rows_b, members
    )
    kept_b = list(kept_b)
    pulled_a[0], kept_b[0] = after(pulled_a[0], kept_b[0])
    pulls_a = pair_pull(pulled_a)
    back_a = give_back(pulls_a)
    kept_b[3], back_a[0] = after(kept_b[3], back_a[0])
    late, sends = finish(
        info, mixed, kept_b[3], weight_in, weight_down, head_t, target_t, rows_b, members
    )
    pulled_b = exchange(sends)
    saved = [list(kept_a), kept_b + list(late)]
    attract_a, late_hidden = after(saved[0][6], saved[1][5])
    saved[1][5] = late_hidden
    grads = [
        slopes(
            info, attract_a, back_a, head_t, weight_down, saved[0][4], scale, share
        )
    ]
    pulled_b[0], ghid = after(pulled_b[0], grads[0][1])
    grads[0] = [grads[0][0], ghid, grads[0][2]]
    pulls_b = list(pair_pull(pulled_b))
    back_b = give_back(pulls_b)
    gpre_a, back_b[0] = after(grads[0][2], back_b[0])
    smalls = [
        norms(gpre_a, weight_in, saved[0][1], saved[0][2], gain, mixed, (), rows_a)
    ]
    attract_b, smalls[0] = after(saved[1][6], smalls[0])
    grads.append(
        slopes(info, attract_b, back_b, head_t, weight_down, saved[1][4], scale, share)
    )

    hids = [saved[h][5] for h in range(2)]
    depths = spaces.bit_length() - 2
    rows, edges = halves[1]
    normal, inv = saved[1][1:3]
    smalls.append(norms(grads[1][2], weight_in, normal, inv, gain, mixed, edges, rows))
    keep_h, send_h = heads(info, [grads[h][0] for h in range(2)], hids, smalls, devices)
    got_h = start_blocks(send_h)
    keep_d, send_d = weights(
        info, [saved[h][3] for h in range(2)], [grads[h][1] for h in range(2)], devices
    )
    got_d = start_blocks(send_d)
    flows_h, flows_d = flows_of(keep_h.shape[1]), flows_of(keep_d.shape[1])
    keep_h, keep_d = after(keep_h, keep_d)
    part_h = merge_blocks(info, [keep_h], [got_h], flows_h, 0)
    gpre = [grads[h][2] for h in range(2)]
    gpre[1], part_h[0][0] = after(gpre[1], part_h[0][0])
    keep_i, send_i = weights(info, gpre, [saved[h][0] for h in range(2)], devices)
    got_i = start_blocks(send_i)
    part_h[0][0], keep_i = after(part_h[0][0], keep_i)
    for depth in range(1, depths):
        part_h = merge_blocks(info, *part_h, flows_h, depth)
    keep_d, part_h[0][0] = after(keep_d, part_h[0][0])
    part_d = [keep_d] * len(flows_d), [got_d] * len(flows_d)
    part_d = merge_blocks(info, *part_d, flows_d, 0)
    keep_i, part_d[0][0] = after(keep_i, part_d[0][0])
    part_i = [keep_i] * len(flows_d), [got_i] * len(flows_d)
    part_i = merge_blocks(info, *part_i, flows_d, 0)
    part_h[0][0], part_i[0][0] = after(part_h[0][0], part_i[0][0])
    own_h, others_h = fold_members(info, part_h[0][0], part_h[1][0])
    part_d[0][0], own_h = after(part_d[0][0], own_h)
    for depth in range(1, depths):
        part_d = merge_blocks(info, *part_d, flows_d, depth)
    own_h, part_d[0][0] = after(own_h, part_d[0][0])
    whole = fold(info, [own_h, *others_h])[None]
    bit = spaces // 2
    part_i[0][0], whole = after(part_i[0][0], whole)
    whole = spread_step(whole, bit)
    for depth in range(1, depths):
        part_i = merge_blocks(info, *part_i, flows_d, depth)
    part_d[0][0], part_i[0][0] = after(part_d[0][0], part_i[0][0])
    own_d, others_d = turn_blocks(info, *part_d)
    part_i[0][0], own_d = after(part_i[0][0], own_d)
    whole, own_d = after(whole, own_d)
    while bit > 2:
        bit //= 2
        whole = spread_step(whole, bit)
    own_i, others_i = turn_blocks(info, *part_i)
    whole, own_i = after(whole, own_i)
    whole = spread_step(whole, 1)
    units = weight_in.shape[0] // devices
    head_total, conv_total, gain_total = placed(info, whole, out_width)
    own_i, head_total = after(own_i, head_total)
    in_mine = add_up(own_i, others_i)[:units]
    down_mine = add_up(own_d, others_d)[:units]
    return (in_mine, down_mine, head_total.T, gain_total.reshape(width), conv_total)


def solution(mesh):
    return jax.shard_map(
        body,
        mesh=mesh,
        in_specs=(
            P("space", None, None),
            P("member", "space", None, None),
            P(),
            P(),
            P(),
            P(),
            P(),
            P("space", None, None),
        ),
        out_specs=(P(("member", "space"), None), P(("member", "space"), None), P(), P(), P()),
        check_vma=False,
    )
```
